128 devices in a mesh: row: 8 (over x, z_lo), col: 16 (over y, z_hi, core).
Axes of the slice: x: 4, y: 4, z: 4 (z_hi: 2, z_lo: 2; z = z_hi * 2 + z_lo), core: 2. Of those that a mesh axis runs over, the one named last changes fastest.
Arguments:
- tokens_in: bfloat16 [8192, 5120], P('row', 'col'), may hold values from -6 to 6
- token_grad: bfloat16 [8192, 5120], P('row', 'col'), may hold values from -6 to 6
- gate_gain: float32 [5120], replicated, may hold values from -4 to 4
- inner_weight: bfloat16 [5120, 13824], P(None, 'col'), may hold values from -0.078125 to 0.078125
- inner_bias: float32 [13824], P('col'), may hold values from -4 to 4
- outer_weight: bfloat16 [5120, 13824], P(None, 'col'), may hold values from -0.0546875 to 0.0546875
- inner_down: bfloat16 [5120, 64], replicated, may hold values from -0.078125 to 0.078125
- inner_up: bfloat16 [64, 13824], P(None, 'col'), may hold values from -0.1796875 to 0.1796875
- outer_down: bfloat16 [13824, 64], P('col'), may hold values from -0.0546875 to 0.0546875
- outer_up: bfloat16 [64, 5120], replicated, may hold values from -0.1796875 to 0.1796875
Outputs:
- tokens_grad: bfloat16 [8192, 5120], P('row', 'col')
- inner_down_grad: float32 [5120, 64], P('col')
- inner_up_grad: float32 [64, 13824], P(None, 'col')
- outer_down_grad: float32 [13824, 64], P('col')
- outer_up_grad: float32 [64, 5120], P(None, 'col')
The draws below stay inside these ranges and needn't reach their ends.
All inputs are finite; a program needn't handle non-finite values.
Results may differ from the reference program's by a relative error of at most 0.023.
Values may be sent and summed in bfloat16 or wider, within the bound.
A program may use at most 128 MiB of HBM per device.

```python
import math
import jax
import jax.numpy as jnp
from jax import lax

D = 5120
FF = 13824
R = 64
TOKENS = 8192
FF_BLOCK = 864
N_COL = 16


def level_of(rng, shape, pieces, smallest, largest):
    gain, own = 1.0, jax.random.fold_in(rng, 6)
    for position, parts in pieces:
        draws = jnp.exp(jax.random.uniform(jax.random.fold_in(own, position), (parts,), jnp.float32, smallest / len(pieces), largest / len(pieces)))
        gain = gain * jnp.repeat(draws, shape[position] // parts).reshape([-1 if axis == position else 1 for axis in range(len(shape))])
    return gain


def normal_values(key, dims, width, reach, split=(), held_as=jnp.bfloat16):
    entries = width * jax.random.normal(key, dims, jnp.float32)
    if split:
        entries = entries * level_of(key, dims, split, -0.22, 0.18)
    return jnp.clip(entries, -reach, reach).astype(held_as)


def setup_inputs(seed: int = 0) -> dict:
    arg_keys = jax.random.split(jax.random.key(seed), 11)
    tokens_in = normal_values(arg_keys[0], (TOKENS, D), 1.0, 6.0, ((0, 8), (1, 16)))
    token_grad = normal_values(arg_keys[1], (TOKENS, D), 1.0, 6.0, ((0, 8), (1, 16)))
    gate_gain = normal_values(arg_keys[2], (D,), 1.0, 4.0, (), jnp.float32)
    inner_weight = normal_values(arg_keys[3], (D, FF), D ** -0.5, 0.078125, ((1, 16),))
    inner_bias = normal_values(arg_keys[4], (FF,), 1.0, 4.0, ((0, 16),), jnp.float32)
    outer_weight = normal_values(arg_keys[5], (D, FF), FF ** -0.5, 0.0546875, ((1, 16),))
    inner_down = normal_values(arg_keys[6], (D, R), D ** -0.5, 0.078125)
    inner_up = normal_values(arg_keys[7], (R, FF), 0.03, 0.1796875, ((1, 16),))
    outer_down = normal_values(arg_keys[8], (FF, R), FF ** -0.5, 0.0546875, ((0, 16),))
    outer_up = normal_values(arg_keys[9], (R, D), 0.03, 0.1796875)
    return dict(tokens_in=tokens_in, token_grad=token_grad, gate_gain=gate_gain, inner_weight=inner_weight, inner_bias=inner_bias, outer_weight=outer_weight, inner_down=inner_down, inner_up=inner_up, outer_down=outer_down, outer_up=outer_up)


SLOPE_SCALE = 0.7978845608028654
CUBIC = 0.044715

def gelu_value(pre):
    inner = SLOPE_SCALE * (pre + CUBIC * pre * pre * pre)
    return 0.5 * pre * (1.0 + jnp.tanh(inner))

def gelu_slope(pre):
    tangent = jnp.tanh(SLOPE_SCALE * (pre + CUBIC * pre * pre * pre))
    return 0.5 * (1.0 + tangent) + 0.5 * pre * (1.0 - tangent * tangent) * SLOPE_SCALE * (1.0 + 3.0 * CUBIC * pre * pre)

def reference(tokens_in, token_grad, gate_gain, inner_weight, inner_bias, outer_weight, inner_down, inner_up, outer_down, outer_up):
    f32 = jnp.float32
    bf16 = jnp.bfloat16
    gated = (gate_gain[None, :] * token_grad.astype(f32)).astype(bf16)
    inner_low = jnp.dot(tokens_in, inner_down, preferred_element_type=f32).astype(bf16)
    pre = jnp.dot(tokens_in, inner_weight, preferred_element_type=f32) + jnp.dot(inner_low, inner_up, preferred_element_type=f32) + inner_bias[None, :]
    hidden = gelu_value(pre).astype(bf16)
    hidden_low = jnp.dot(hidden, outer_down, preferred_element_type=f32).astype(bf16)
    grad_low = jnp.dot(gated, outer_up.T, preferred_element_type=f32).astype(bf16)
    grad_hidden = jnp.dot(gated, outer_weight, preferred_element_type=f32) + jnp.dot(grad_low, outer_down.T, preferred_element_type=f32)
    grad_pre = (grad_hidden * gelu_slope(pre)).astype(bf16)
    pre_low = jnp.dot(grad_pre, inner_up.T, preferred_element_type=f32).astype(bf16)

    def add_block(total, index):
        start = index * FF_BLOCK
        piece = lax.dynamic_slice_in_dim(grad_pre, start, FF_BLOCK, 1)
        weights = lax.dynamic_slice_in_dim(inner_weight, start, FF_BLOCK, 1)
        part = jnp.dot(piece, weights.T, preferred_element_type=f32).astype(bf16)
        part = lax.optimization_barrier(part)
        return (total + part.astype(f32), None)
    start_total = jnp.zeros((tokens_in.shape[0], tokens_in.shape[1]), f32)
    total, _ = lax.scan(add_block, start_total, jnp.arange(N_COL, dtype=jnp.int32))
    tokens_grad = (total + jnp.dot(pre_low, inner_down.T, preferred_element_type=f32)).astype(bf16)
    scale = 1.0 / math.sqrt(tokens_in.shape[0])
    inner_down_grad = jnp.dot(tokens_in.T, pre_low, preferred_element_type=f32) * scale
    inner_up_grad = jnp.dot(inner_low.T, grad_pre, preferred_element_type=f32) * scale
    outer_down_grad = jnp.dot(hidden.T, grad_low, preferred_element_type=f32) * scale
    outer_up_grad = jnp.dot(hidden_low.T, gated, preferred_element_type=f32) * scale
    return (tokens_grad, inner_down_grad, inner_up_grad, outer_down_grad, outer_up_grad)
```

```python
import math

import jax
import jax.numpy as jnp
from jax import lax
from jax.sharding import PartitionSpec as P

SLOPE_SCALE = 0.7978845608028654
CUBIC = 0.044715


def gelu_value(pre):
    inner = SLOPE_SCALE * (pre + CUBIC * pre * pre * pre)
    return 0.5 * pre * (1.0 + jnp.tanh(inner))


def gelu_slope(pre):
    tangent = jnp.tanh(SLOPE_SCALE * (pre + CUBIC * pre * pre * pre))
    return 0.5 * (1.0 + tangent) + 0.5 * pre * (1.0 - tangent * tangent) * SLOPE_SCALE * (
        1.0 + 3.0 * CUBIC * pre * pre
    )


def plain_dot(left, right):
    return jnp.dot(left, right, preferred_element_type=jnp.float32)


def dot_rows(left, right):
    return lax.dot_general(
        left, right, (((1,), (1,)), ((), ())), preferred_element_type=jnp.float32
    )


def dot_cols(left, right):
    return lax.dot_general(
        left, right, (((0,), (0,)), ((), ())), preferred_element_type=jnp.float32
    )


def tree_sum(value, axis, size):
    step = 1
    while step < size:
        pairs = [(i, i ^ step) for i in range(size)]
        value = value + lax.ppermute(value, axis, pairs)
        step *= 2
    return value


def local(
    tokens_in,
    token_grad,
    gate_gain,
    inner_weight,
    inner_bias,
    outer_weight,
    inner_down,
    inner_up,
    outer_down,
    outer_up,
):
    n_col = lax.axis_size("col")
    n_row = lax.axis_size("row")
    col_index = lax.axis_index("col")
    local_width = token_grad.shape[1]
    tok_rows = tokens_in.shape[0]
    ff_local = inner_weight.shape[1]
    rank = inner_down.shape[1]
    gain_local = lax.dynamic_slice_in_dim(gate_gain, col_index * local_width, local_width, 0)
    gated_local = (gain_local[None, :] * token_grad.astype(jnp.float32)).astype(jnp.bfloat16)
    tokens_full = lax.all_gather(tokens_in, "col", axis=1, tiled=True)
    gated_full = lax.all_gather(gated_local, "col", axis=1, tiled=True)
    inner_low = plain_dot(tokens_full, inner_down).astype(jnp.bfloat16)
    forward_sum = plain_dot(tokens_full, inner_weight)
    grad_low = dot_rows(gated_full, outer_up).astype(jnp.bfloat16)
    backward_sum = plain_dot(gated_full, outer_weight)
    pre = forward_sum + plain_dot(inner_low, inner_up) + inner_bias[None, :]
    hidden = gelu_value(pre).astype(jnp.bfloat16)
    grad_hidden = backward_sum + dot_rows(grad_low, outer_down)
    grad_pre = (grad_hidden * gelu_slope(pre)).astype(jnp.bfloat16)
    pre_low_part = dot_rows(grad_pre, inner_up)
    block_part = dot_rows(grad_pre, inner_weight).astype(jnp.bfloat16).astype(jnp.float32)
    low_part = dot_rows(pre_low_part.astype(jnp.bfloat16), inner_down)
    tokens_grad = lax.psum_scatter(
        (block_part + low_part).astype(jnp.bfloat16), "col", scatter_dimension=1, tiled=True
    )

    hidden_low_part = plain_dot(hidden, outer_down)
    lows = tree_sum(jnp.concatenate([hidden_low_part, pre_low_part], axis=1), "col", n_col)
    hidden_low = lows[:, :rank].astype(jnp.bfloat16)
    pre_low = lows[:, rank:].astype(jnp.bfloat16)

    scale = 1.0 / math.sqrt(tok_rows * n_row)
    outer_down_term = dot_cols(hidden, grad_low)
    outer_up_term = dot_cols(gated_local, hidden_low)
    inner_down_term = dot_cols(tokens_in, pre_low)
    inner_up_term = dot_cols(grad_pre, inner_low)
    packed = jnp.concatenate([outer_down_term, inner_up_term, outer_up_term, inner_down_term], axis=0)
    packed = tree_sum(packed, "row", n_row) * scale
    outer_down_grad = packed[:ff_local]
    inner_up_grad = packed[ff_local : 2 * ff_local].T
    outer_up_grad = packed[2 * ff_local : 2 * ff_local + local_width].T
    inner_down_grad = packed[2 * ff_local + local_width :]
    return (tokens_grad, inner_down_grad, inner_up_grad, outer_down_grad, outer_up_grad)


def solution(mesh):
    placed = (
        P("row", "col"),
        P("row", "col"),
        P(),
        P(None, "col"),
        P("col"),
        P(None, "col"),
        P(),
        P(None, "col"),
        P("col", None),
        P(),
    )
    return jax.shard_map(
        local,
        mesh=mesh,
        in_specs=placed,
        out_specs=(P("row", "col"), P("col", None), P(None, "col"), P("col", None), P(None, "col")),
        check_vma=False,
    )
```

```python
import math

import jax
import jax.numpy as jnp
from jax import lax
from jax.sharding import Mesh
from jax.sharding import PartitionSpec as P

SLOPE_SCALE = 0.7978845608028654
CUBIC = 0.044715
COL = ("cc", "core")


def gelu_value(pre):
    inner = SLOPE_SCALE * (pre + CUBIC * pre * pre * pre)
    return 0.5 * pre * (1.0 + jnp.tanh(inner))


def gelu_slope(pre):
    tangent = jnp.tanh(SLOPE_SCALE * (pre + CUBIC * pre * pre * pre))
    return 0.5 * (1.0 + tangent) + 0.5 * pre * (1.0 - tangent * tangent) * SLOPE_SCALE * (
        1.0 + 3.0 * CUBIC * pre * pre
    )


def plain_dot(left, right):
    return jnp.dot(left, right, preferred_element_type=jnp.float32)


def dot_rows(left, right):
    return lax.dot_general(
        left, right, (((1,), (1,)), ((), ())), preferred_element_type=jnp.float32
    )


def dot_cols(left, right):
    return lax.dot_general(
        left, right, (((0,), (0,)), ((), ())), preferred_element_type=jnp.float32
    )


def tree_sum(value, axis, size):
    step = 1
    while step < size:
        pairs = [(i, i ^ step) for i in range(size)]
        value = value + lax.ppermute(value, axis, pairs)
        step *= 2
    return value


def core_major(rows, n_cc, n_core):
    shape = rows.shape
    split = rows.reshape((n_cc, n_core, shape[0] // (n_cc * n_core)) + shape[1:])
    return jnp.swapaxes(split, 0, 1).reshape(shape)


def gather_features(block, n_cc, n_core):
    over_chips = lax.all_gather(block, "cc", axis=1, tiled=True)
    return lax.all_gather(over_chips, "core", axis=1, tiled=True)


def local(
    tokens_in,
    token_grad,
    gate_gain,
    inner_weight,
    inner_bias,
    outer_weight,
    inner_down,
    inner_up,
    outer_down,
    outer_up,
):
    n_cc = lax.axis_size("cc")
    n_core = lax.axis_size("core")
    n_col = n_cc * n_core
    n_row = lax.axis_size("row")
    col_index = lax.axis_index("cc") * n_core + lax.axis_index("core")
    local_width = token_grad.shape[1]
    tok_rows = tokens_in.shape[0]
    ff_local = inner_weight.shape[1]
    rank = inner_down.shape[1]
    gain_local = lax.dynamic_slice_in_dim(gate_gain, col_index * local_width, local_width, 0)
    gated_local = (gain_local[None, :] * token_grad.astype(jnp.float32)).astype(jnp.bfloat16)
    tokens_full = gather_features(tokens_in, n_cc, n_core)
    gated_full = gather_features(gated_local, n_cc, n_core)
    inner_weight_p = core_major(inner_weight, n_cc, n_core)
    outer_weight_p = core_major(outer_weight, n_cc, n_core)
    inner_down_p = core_major(inner_down, n_cc, n_core)
    outer_up_p = core_major(outer_up.T, n_cc, n_core)

    inner_low = plain_dot(tokens_full, inner_down_p).astype(jnp.bfloat16)
    forward_sum = plain_dot(tokens_full, inner_weight_p)
    grad_low = plain_dot(gated_full, outer_up_p).astype(jnp.bfloat16)
    backward_sum = plain_dot(gated_full, outer_weight_p)
    pre = forward_sum + plain_dot(inner_low, inner_up) + inner_bias[None, :]
    hidden = gelu_value(pre).astype(jnp.bfloat16)
    grad_hidden = backward_sum + dot_rows(grad_low, outer_down)
    grad_pre = (grad_hidden * gelu_slope(pre)).astype(jnp.bfloat16)
    pre_low_part = dot_rows(grad_pre, inner_up)
    block_part = dot_rows(grad_pre, inner_weight_p).astype(jnp.bfloat16).astype(jnp.float32)
    low_part = dot_rows(pre_low_part.astype(jnp.bfloat16), inner_down_p)
    summed = (block_part + low_part).astype(jnp.bfloat16)
    on_chip = lax.psum_scatter(summed, "core", scatter_dimension=1, tiled=True)
    tokens_grad = lax.psum_scatter(on_chip, "cc", scatter_dimension=1, tiled=True)

    hidden_low_part = plain_dot(hidden, outer_down)
    lows = tree_sum(jnp.concatenate([hidden_low_part, pre_low_part], axis=1), COL, n_col)
    hidden_low = lows[:, :rank].astype(jnp.bfloat16)
    pre_low = lows[:, rank:].astype(jnp.bfloat16)

    scale = 1.0 / math.sqrt(tok_rows * n_row)
    outer_down_term = dot_cols(hidden, grad_low)
    outer_up_term = dot_cols(gated_local, hidden_low)
    inner_down_term = dot_cols(tokens_in, pre_low)
    inner_up_term = dot_cols(grad_pre, inner_low)
    packed = jnp.concatenate([outer_down_term, inner_up_term, outer_up_term, inner_down_term], axis=0)
    packed = tree_sum(packed, "row", n_row) * scale
    outer_down_grad = packed[:ff_local]
    inner_up_grad = packed[ff_local : 2 * ff_local].T
    outer_up_grad = packed[2 * ff_local : 2 * ff_local + local_width].T
    inner_down_grad = packed[2 * ff_local + local_width :]
    return (tokens_grad, inner_down_grad, inner_up_grad, outer_down_grad, outer_up_grad)


def solution(mesh):
    n_row, n_col = mesh.devices.shape
    split = Mesh(mesh.devices.reshape(n_row, n_col // 2, 2), ("row", "cc", "core"))
    placed = (
        P("row", COL),
        P("row", COL),
        P(),
        P(None, COL),
        P(COL),
        P(None, COL),
        P(),
        P(None, COL),
        P(COL, None),
        P(),
    )
    return jax.shard_map(
        local,
        mesh=split,
        in_specs=placed,
        out_specs=(P("row", COL), P(COL, None), P(None, COL), P(COL, None), P(None, COL)),
        check_vma=False,
    )
```

```python
import functools
import math

import jax
import jax.numpy as jnp
from jax import lax
from jax.experimental import pallas as pl
from jax.experimental.pallas import tpu as pltpu
from jax.sharding import PartitionSpec as P

MESH = pl.DeviceIdType.MESH

SLOPE_SCALE = 0.7978845608028654
CUBIC = 0.044715


def gelu_value(pre):
    inner = SLOPE_SCALE * (pre + CUBIC * pre * pre * pre)
    return 0.5 * pre * (1.0 + jnp.tanh(inner))


def gelu_slope(pre):
    tangent = jnp.tanh(SLOPE_SCALE * (pre + CUBIC * pre * pre * pre))
    return 0.5 * (1.0 + tangent) + 0.5 * pre * (1.0 - tangent * tangent) * SLOPE_SCALE * (
        1.0 + 3.0 * CUBIC * pre * pre
    )


def plain_dot(left, right):
    return jnp.dot(left, right, preferred_element_type=jnp.float32)


def dot_rows(left, right):
    return lax.dot_general(
        left, right, (((1,), (1,)), ((), ())), preferred_element_type=jnp.float32
    )


def dot_cols(left, right):
    return lax.dot_general(
        left, right, (((0,), (0,)), ((), ())), preferred_element_type=jnp.float32
    )


def tree_sum(value, axis, size):
    step = 1
    while step < size:
        pairs = [(i, i ^ step) for i in range(size)]
        value = value + lax.ppermute(value, axis, pairs)
        step *= 2
    return value


def gather_kernel(n, x_ref, out_ref, own_sem, send_sem, recv_sem):
    me = lax.axis_index("col")
    row = lax.axis_index("row")
    barrier = pltpu.get_barrier_semaphore()
    for k in range(1, n):
        peer = lax.rem(me + k, n)
        pl.semaphore_signal(barrier, inc=1, device_id=(row, peer), device_id_type=MESH)
    pl.semaphore_wait(barrier, n - 1)
    own = pltpu.make_async_copy(x_ref, out_ref.at[me], own_sem)
    own.start()
    sends = []
    for k in range(1, n):
        peer = lax.rem(me + k, n)
        copy = pltpu.make_async_remote_copy(
            src_ref=x_ref,
            dst_ref=out_ref.at[me],
            send_sem=send_sem.at[k],
            recv_sem=recv_sem.at[k],
            device_id=(row, peer),
            device_id_type=MESH,
        )
        copy.start()
        sends.append(copy)
    own.wait()
    for copy in sends:
        copy.wait_send()
    for k in range(1, n):
        source = lax.rem(me + n - k, n)
        pltpu.make_async_remote_copy(
            src_ref=x_ref,
            dst_ref=out_ref.at[source],
            send_sem=send_sem.at[k],
            recv_sem=recv_sem.at[k],
            device_id=(row, source),
            device_id_type=MESH,
        ).wait_recv()


def gather_blocks(block, n, collective_id):
    rows, width = block.shape
    nbytes = rows * width * block.dtype.itemsize
    return pl.pallas_call(
        functools.partial(gather_kernel, n),
        out_shape=jax.ShapeDtypeStruct((n, rows, width), block.dtype),
        in_specs=[pl.BlockSpec(memory_space=pltpu.VMEM)],
        out_specs=pl.BlockSpec(memory_space=pl.ANY),
        scratch_shapes=[
            pltpu.SemaphoreType.DMA(()),
            pltpu.SemaphoreType.DMA((n,)),
            pltpu.SemaphoreType.DMA((n,)),
        ],
        compiler_params=pltpu.CompilerParams(collective_id=collective_id, has_side_effects=True),
        cost_estimate=pl.CostEstimate(flops=0, transcendentals=0, bytes_accessed=2 * n * nbytes),
    )(block)


def local(
    tokens_in,
    token_grad,
    gate_gain,
    inner_weight,
    inner_bias,
    outer_weight,
    inner_down,
    inner_up,
    outer_down,
    outer_up,
):
    n_col = lax.axis_size("col")
    n_row = lax.axis_size("row")
    col_index = lax.axis_index("col")
    local_width = token_grad.shape[1]
    tok_rows = tokens_in.shape[0]
    ff_local = inner_weight.shape[1]
    rank = inner_down.shape[1]
    gain_local = lax.dynamic_slice_in_dim(gate_gain, col_index * local_width, local_width, 0)
    gated_local = (gain_local[None, :] * token_grad.astype(jnp.float32)).astype(jnp.bfloat16)
    tokens_blocks = gather_blocks(tokens_in, n_col, 0)
    tokens_full = jnp.swapaxes(tokens_blocks, 0, 1).reshape(tok_rows, n_col * local_width)
    gated_full = lax.all_gather(gated_local, "col", axis=1, tiled=True)
    inner_low = plain_dot(tokens_full, inner_down).astype(jnp.bfloat16)
    forward_sum = plain_dot(tokens_full, inner_weight)
    grad_low = dot_rows(gated_full, outer_up).astype(jnp.bfloat16)
    backward_sum = plain_dot(gated_full, outer_weight)
    pre = forward_sum + plain_dot(inner_low, inner_up) + inner_bias[None, :]
    hidden = gelu_value(pre).astype(jnp.bfloat16)
    grad_hidden = backward_sum + dot_rows(grad_low, outer_down)
    grad_pre = (grad_hidden * gelu_slope(pre)).astype(jnp.bfloat16)
    pre_low_part = dot_rows(grad_pre, inner_up)
    block_part = dot_rows(grad_pre, inner_weight).astype(jnp.bfloat16).astype(jnp.float32)
    low_part = dot_rows(pre_low_part.astype(jnp.bfloat16), inner_down)
    tokens_grad = lax.psum_scatter(
        (block_part + low_part).astype(jnp.bfloat16), "col", scatter_dimension=1, tiled=True
    )

    hidden_low_part = plain_dot(hidden, outer_down)
    lows = tree_sum(jnp.concatenate([hidden_low_part, pre_low_part], axis=1), "col", n_col)
    hidden_low = lows[:, :rank].astype(jnp.bfloat16)
    pre_low = lows[:, rank:].astype(jnp.bfloat16)

    scale = 1.0 / math.sqrt(tok_rows * n_row)
    outer_down_term = dot_cols(hidden, grad_low)
    outer_up_term = dot_cols(gated_local, hidden_low)
    inner_down_term = dot_cols(tokens_in, pre_low)
    inner_up_term = dot_cols(grad_pre, inner_low)
    packed = jnp.concatenate([outer_down_term, inner_up_term, outer_up_term, inner_down_term], axis=0)
    packed = tree_sum(packed, "row", n_row) * scale
    outer_down_grad = packed[:ff_local]
    inner_up_grad = packed[ff_local : 2 * ff_local].T
    outer_up_grad = packed[2 * ff_local : 2 * ff_local + local_width].T
    inner_down_grad = packed[2 * ff_local + local_width :]
    return (tokens_grad, inner_down_grad, inner_up_grad, outer_down_grad, outer_up_grad)


def solution(mesh):
    placed = (
        P("row", "col"),
        P("row", "col"),
        P(),
        P(None, "col"),
        P("col"),
        P(None, "col"),
        P(),
        P(None, "col"),
        P("col", None),
        P(),
    )
    return jax.shard_map(
        local,
        mesh=mesh,
        in_specs=placed,
        out_specs=(P("row", "col"), P("col", None), P(None, "col"), P("col", None), P(None, "col")),
        check_vma=False,
    )
```

```python
import math

import jax
import jax.numpy as jnp
from jax import lax
from jax.sharding import PartitionSpec as P

SLOPE_SCALE = 0.7978845608028654
CUBIC = 0.044715


def gelu_value(pre):
    inner = SLOPE_SCALE * (pre + CUBIC * pre * pre * pre)
    return 0.5 * pre * (1.0 + jnp.tanh(inner))


def gelu_slope(pre):
    tangent = jnp.tanh(SLOPE_SCALE * (pre + CUBIC * pre * pre * pre))
    return 0.5 * (1.0 + tangent) + 0.5 * pre * (1.0 - tangent * tangent) * SLOPE_SCALE * (
        1.0 + 3.0 * CUBIC * pre * pre
    )


def plain_dot(left, right):
    return jnp.dot(left, right, preferred_element_type=jnp.float32)


def dot_rows(left, right):
    return lax.dot_general(
        left, right, (((1,), (1,)), ((), ())), preferred_element_type=jnp.float32
    )


def dot_cols(left, right):
    return lax.dot_general(
        left, right, (((0,), (0,)), ((), ())), preferred_element_type=jnp.float32
    )


def tree_sum(value, axis, size):
    step = 1
    while step < size:
        pairs = [(i, i ^ step) for i in range(size)]
        value = value + lax.ppermute(value, axis, pairs)
        step *= 2
    return value


def local(
    tokens_in,
    token_grad,
    gate_gain,
    inner_weight,
    inner_bias,
    outer_weight,
    inner_down,
    inner_up,
    outer_down,
    outer_up,
):
    n_col = lax.axis_size("col")
    n_row = lax.axis_size("row")
    col_index = lax.axis_index("col")
    local_width = token_grad.shape[1]
    tok_rows = tokens_in.shape[0]
    ff_local = inner_weight.shape[1]
    rank = inner_down.shape[1]
    gain_local = lax.dynamic_slice_in_dim(gate_gain, col_index * local_width, local_width, 0)
    gated_local = (gain_local[None, :] * token_grad.astype(jnp.float32)).astype(jnp.bfloat16)
    tokens_full = lax.all_gather(tokens_in, "col", axis=1, tiled=True)
    inner_low = plain_dot(tokens_full, inner_down).astype(jnp.bfloat16)
    pre = plain_dot(tokens_full, inner_weight) + plain_dot(inner_low, inner_up) + inner_bias[None, :]
    hidden = gelu_value(pre).astype(jnp.bfloat16)

    half = tok_rows // 2
    grad_lows, grad_pres, pre_low_parts, grads = [], [], [], []
    for lo in (0, half):
        gated_part = lax.all_gather(gated_local[lo : lo + half], "col", axis=1, tiled=True)
        grad_low = dot_rows(gated_part, outer_up).astype(jnp.bfloat16)
        grad_hidden = plain_dot(gated_part, outer_weight) + dot_rows(grad_low, outer_down)
        grad_pre = (grad_hidden * gelu_slope(pre[lo : lo + half])).astype(jnp.bfloat16)
        pre_low_part = dot_rows(grad_pre, inner_up)
        block_part = dot_rows(grad_pre, inner_weight).astype(jnp.bfloat16).astype(jnp.float32)
        low_part = dot_rows(pre_low_part.astype(jnp.bfloat16), inner_down)
        grads.append(
            lax.psum_scatter(
                (block_part + low_part).astype(jnp.bfloat16), "col", scatter_dimension=1, tiled=True
            )
        )
        grad_lows.append(grad_low)
        grad_pres.append(grad_pre)
        pre_low_parts.append(pre_low_part)
    tokens_grad = jnp.concatenate(grads, axis=0)
    grad_low = jnp.concatenate(grad_lows, axis=0)
    grad_pre = jnp.concatenate(grad_pres, axis=0)
    pre_low_part = jnp.concatenate(pre_low_parts, axis=0)

    hidden_low_part = plain_dot(hidden, outer_down)
    lows = tree_sum(jnp.concatenate([hidden_low_part, pre_low_part], axis=1), "col", n_col)
    hidden_low = lows[:, :rank].astype(jnp.bfloat16)
    pre_low = lows[:, rank:].astype(jnp.bfloat16)

    scale = 1.0 / math.sqrt(tok_rows * n_row)
    outer_down_term = dot_cols(hidden, grad_low)
    outer_up_term = dot_cols(gated_local, hidden_low)
    inner_down_term = dot_cols(tokens_in, pre_low)
    inner_up_term = dot_cols(grad_pre, inner_low)
    packed = jnp.concatenate([outer_down_term, inner_up_term, outer_up_term, inner_down_term], axis=0)
    packed = tree_sum(packed, "row", n_row) * scale
    outer_down_grad = packed[:ff_local]
    inner_up_grad = packed[ff_local : 2 * ff_local].T
    outer_up_grad = packed[2 * ff_local : 2 * ff_local + local_width].T
    inner_down_grad = packed[2 * ff_local + local_width :]
    return (tokens_grad, inner_down_grad, inner_up_grad, outer_down_grad, outer_up_grad)


def solution(mesh):
    placed = (
        P("row", "col"),
        P("row", "col"),
        P(),
        P(None, "col"),
        P("col"),
        P(None, "col"),
        P(),
        P(None, "col"),
        P("col", None),
        P(),
    )
    return jax.shard_map(
        local,
        mesh=mesh,
        in_specs=placed,
        out_specs=(P("row", "col"), P("col", None), P(None, "col"), P("col", None), P(None, "col")),
        check_vma=False,
    )
```

```python
import math

import jax
import jax.numpy as jnp
from jax import lax
from jax.sharding import PartitionSpec as P

SLOPE_SCALE = 0.7978845608028654
CUBIC = 0.044715


def gelu_value(pre):
    inner = SLOPE_SCALE * (pre + CUBIC * pre * pre * pre)
    return 0.5 * pre * (1.0 + jnp.tanh(inner))


def gelu_slope(pre):
    tangent = jnp.tanh(SLOPE_SCALE * (pre + CUBIC * pre * pre * pre))
    return 0.5 * (1.0 + tangent) + 0.5 * pre * (1.0 - tangent * tangent) * SLOPE_SCALE * (
        1.0 + 3.0 * CUBIC * pre * pre
    )


def plain_dot(left, right):
    return jnp.dot(left, right, preferred_element_type=jnp.float32)


def dot_rows(left, right):
    return lax.dot_general(
        left, right, (((1,), (1,)), ((), ())), preferred_element_type=jnp.float32
    )


def dot_cols(left, right):
    return lax.dot_general(
        left, right, (((0,), (0,)), ((), ())), preferred_element_type=jnp.float32
    )


def tree_sum(value, axis, size):
    step = 1
    while step < size:
        pairs = [(i, i ^ step) for i in range(size)]
        value = value + lax.ppermute(value, axis, pairs)
        step *= 2
    return value


def local(
    tokens_in,
    token_grad,
    gate_gain,
    inner_weight,
    inner_bias,
    outer_weight,
    inner_down,
    inner_up,
    outer_down,
    outer_up,
):
    n_col = lax.axis_size("col")
    n_row = lax.axis_size("row")
    col_index = lax.axis_index("col")
    local_width = token_grad.shape[1]
    tok_rows = tokens_in.shape[0]
    ff_local = inner_weight.shape[1]
    rank = inner_down.shape[1]
    gain_local = lax.dynamic_slice_in_dim(gate_gain, col_index * local_width, local_width, 0)
    gated_local = (gain_local[None, :] * token_grad.astype(jnp.float32)).astype(jnp.bfloat16)
    both_full = lax.all_gather(jnp.stack([tokens_in, gated_local]), "col", axis=2, tiled=True)
    tokens_full, gated_full = both_full[0], both_full[1]
    inner_low = plain_dot(tokens_full, inner_down).astype(jnp.bfloat16)
    forward_sum = plain_dot(tokens_full, inner_weight)
    grad_low = dot_rows(gated_full, outer_up).astype(jnp.bfloat16)
    backward_sum = plain_dot(gated_full, outer_weight)
    pre = forward_sum + plain_dot(inner_low, inner_up) + inner_bias[None, :]
    hidden = gelu_value(pre).astype(jnp.bfloat16)
    grad_hidden = backward_sum + dot_rows(grad_low, outer_down)
    grad_pre = (grad_hidden * gelu_slope(pre)).astype(jnp.bfloat16)
    pre_low_part = dot_rows(grad_pre, inner_up)
    block_part = dot_rows(grad_pre, inner_weight).astype(jnp.bfloat16).astype(jnp.float32)
    low_part = dot_rows(pre_low_part.astype(jnp.bfloat16), inner_down)
    tokens_grad = lax.psum_scatter(
        (block_part + low_part).astype(jnp.bfloat16), "col", scatter_dimension=1, tiled=True
    )

    hidden_low_part = plain_dot(hidden, outer_down)
    lows = tree_sum(jnp.concatenate([hidden_low_part, pre_low_part], axis=1), "col", n_col)
    hidden_low = lows[:, :rank].astype(jnp.bfloat16)
    pre_low = lows[:, rank:].astype(jnp.bfloat16)

    scale = 1.0 / math.sqrt(tok_rows * n_row)
    outer_down_term = dot_cols(hidden, grad_low)
    outer_up_term = dot_cols(gated_local, hidden_low)
    inner_down_term = dot_cols(tokens_in, pre_low)
    inner_up_term = dot_cols(grad_pre, inner_low)
    packed = jnp.concatenate([outer_down_term, inner_up_term, outer_up_term, inner_down_term], axis=0)
    packed = tree_sum(packed, "row", n_row) * scale
    outer_down_grad = packed[:ff_local]
    inner_up_grad = packed[ff_local : 2 * ff_local].T
    outer_up_grad = packed[2 * ff_local : 2 * ff_local + local_width].T
    inner_down_grad = packed[2 * ff_local + local_width :]
    return (tokens_grad, inner_down_grad, inner_up_grad, outer_down_grad, outer_up_grad)


def solution(mesh):
    placed = (
        P("row", "col"),
        P("row", "col"),
        P(),
        P(None, "col"),
        P("col"),
        P(None, "col"),
        P(),
        P(None, "col"),
        P("col", None),
        P(),
    )
    return jax.shard_map(
        local,
        mesh=mesh,
        in_specs=placed,
        out_specs=(P("row", "col"), P("col", None), P(None, "col"), P("col", None), P(None, "col")),
        check_vma=False,
    )
```

```python
import math

import jax
import jax.numpy as jnp
from jax import lax
from jax.sharding import PartitionSpec as P

SLOPE_SCALE = 0.7978845608028654
CUBIC = 0.044715


def gelu_value(pre):
    inner = SLOPE_SCALE * (pre + CUBIC * pre * pre * pre)
    return 0.5 * pre * (1.0 + jnp.tanh(inner))


def gelu_slope(pre):
    tangent = jnp.tanh(SLOPE_SCALE * (pre + CUBIC * pre * pre * pre))
    return 0.5 * (1.0 + tangent) + 0.5 * pre * (1.0 - tangent * tangent) * SLOPE_SCALE * (
        1.0 + 3.0 * CUBIC * pre * pre
    )


def plain_dot(left, right):
    return jnp.dot(left, right, preferred_element_type=jnp.float32)


def dot_rows(left, right):
    return lax.dot_general(
        left, right, (((1,), (1,)), ((), ())), preferred_element_type=jnp.float32
    )


def dot_cols(left, right):
    return lax.dot_general(
        left, right, (((0,), (0,)), ((), ())), preferred_element_type=jnp.float32
    )


def tree_sum(value, axis, size):
    step = 1
    while step < size:
        pairs = [(i, i ^ step) for i in range(size)]
        value = value + lax.ppermute(value, axis, pairs)
        step *= 2
    return value


def local(
    tokens_in,
    token_grad,
    gate_gain,
    inner_weight,
    inner_bias,
    outer_weight,
    inner_down,
    inner_up,
    outer_down,
    outer_up,
):
    n_col = lax.axis_size("col")
    n_row = lax.axis_size("row")
    col_index = lax.axis_index("col")
    local_width = token_grad.shape[1]
    tok_rows = tokens_in.shape[0]
    ff_local = inner_weight.shape[1]
    rank = inner_down.shape[1]
    gain_local = lax.dynamic_slice_in_dim(gate_gain, col_index * local_width, local_width, 0)
    gated_local = (gain_local[None, :] * token_grad.astype(jnp.float32)).astype(jnp.bfloat16)
    both_full = lax.all_gather(jnp.stack([tokens_in, gated_local]), "col", axis=2, tiled=True)
    tokens_full, gated_full = both_full[0], both_full[1]
    inner_low = plain_dot(tokens_full, inner_down).astype(jnp.bfloat16)
    forward_sum = plain_dot(tokens_full, inner_weight)
    grad_low = dot_rows(gated_full, outer_up).astype(jnp.bfloat16)
    backward_sum = plain_dot(gated_full, outer_weight)
    pre = forward_sum + plain_dot(inner_low, inner_up) + inner_bias[None, :]
    hidden = gelu_value(pre).astype(jnp.bfloat16)
    grad_hidden = backward_sum + dot_rows(grad_low, outer_down)
    grad_pre = (grad_hidden * gelu_slope(pre)).astype(jnp.bfloat16)
    pre_low_part = dot_rows(grad_pre, inner_up)
    block_part = dot_rows(grad_pre, inner_weight).astype(jnp.bfloat16)
    parts = lax.psum_scatter(block_part, "col", scatter_dimension=1, tiled=True)

    hidden_low_part = plain_dot(hidden, outer_down)
    lows = tree_sum(jnp.concatenate([hidden_low_part, pre_low_part], axis=1), "col", n_col)
    hidden_low = lows[:, :rank].astype(jnp.bfloat16)
    pre_low = lows[:, rank:].astype(jnp.bfloat16)
    down_local = lax.dynamic_slice_in_dim(inner_down, col_index * local_width, local_width, 0)
    tokens_grad = (parts.astype(jnp.float32) + dot_rows(pre_low, down_local)).astype(jnp.bfloat16)

    scale = 1.0 / math.sqrt(tok_rows * n_row)
    outer_down_term = dot_cols(hidden, grad_low)
    outer_up_term = dot_cols(gated_local, hidden_low)
    inner_down_term = dot_cols(tokens_in, pre_low)
    inner_up_term = dot_cols(grad_pre, inner_low)
    packed = jnp.concatenate([outer_down_term, inner_up_term, outer_up_term, inner_down_term], axis=0)
    packed = tree_sum(packed, "row", n_row) * scale
    outer_down_grad = packed[:ff_local]
    inner_up_grad = packed[ff_local : 2 * ff_local].T
    outer_up_grad = packed[2 * ff_local : 2 * ff_local + local_width].T
    inner_down_grad = packed[2 * ff_local + local_width :]
    return (tokens_grad, inner_down_grad, inner_up_grad, outer_down_grad, outer_up_grad)


def solution(mesh):
    placed = (
        P("row", "col"),
        P("row", "col"),
        P(),
        P(None, "col"),
        P("col"),
        P(None, "col"),
        P(),
        P(None, "col"),
        P("col", None),
        P(),
    )
    return jax.shard_map(
        local,
        mesh=mesh,
        in_specs=placed,
        out_specs=(P("row", "col"), P("col", None), P(None, "col"), P("col", None), P(None, "col")),
        check_vma=False,
    )
```

```python
import math

import jax
import jax.numpy as jnp
from jax import lax
from jax.sharding import PartitionSpec as P

SLOPE_SCALE = 0.7978845608028654
CUBIC = 0.044715


def gelu_value(pre):
    inner = SLOPE_SCALE * (pre + CUBIC * pre * pre * pre)
    return 0.5 * pre * (1.0 + jnp.tanh(inner))


def gelu_slope(pre):
    tangent = jnp.tanh(SLOPE_SCALE * (pre + CUBIC * pre * pre * pre))
    return 0.5 * (1.0 + tangent) + 0.5 * pre * (1.0 - tangent * tangent) * SLOPE_SCALE * (
        1.0 + 3.0 * CUBIC * pre * pre
    )


def plain_dot(left, right):
    return jnp.dot(left, right, preferred_element_type=jnp.float32)


def dot_rows(left, right):
    return lax.dot_general(
        left, right, (((1,), (1,)), ((), ())), preferred_element_type=jnp.float32
    )


def dot_cols(left, right):
    return lax.dot_general(
        left, right, (((0,), (0,)), ((), ())), preferred_element_type=jnp.float32
    )


def tree_sum(value, axis, size):
    step = 1
    while step < size:
        pairs = [(i, i ^ step) for i in range(size)]
        value = value + lax.ppermute(value, axis, pairs)
        step *= 2
    return value


def local(
    tokens_in,
    token_grad,
    gate_gain,
    inner_weight,
    inner_bias,
    outer_weight,
    inner_down,
    inner_up,
    outer_down,
    outer_up,
):
    n_col = lax.axis_size("col")
    n_row = lax.axis_size("row")
    col_index = lax.axis_index("col")
    local_width = token_grad.shape[1]
    tok_rows = tokens_in.shape[0]
    ff_local = inner_weight.shape[1]
    rank = inner_down.shape[1]
    gain_local = lax.dynamic_slice_in_dim(gate_gain, col_index * local_width, local_width, 0)
    gated_local = (gain_local[None, :] * token_grad.astype(jnp.float32)).astype(jnp.bfloat16)
    both_full = lax.all_gather(jnp.stack([tokens_in, gated_local]), "col", axis=2, tiled=True)
    tokens_full, gated_full = both_full[0], both_full[1]
    down_local = lax.dynamic_slice_in_dim(inner_down, col_index * local_width, local_width, 0)
    up_local = lax.dynamic_slice_in_dim(outer_up, col_index * local_width, local_width, 1)
    low_parts = jnp.concatenate(
        [plain_dot(tokens_in, down_local), dot_rows(gated_local, up_local)], axis=1
    )
    low_sums = tree_sum(low_parts, "col", n_col)
    inner_low = low_sums[:, :rank].astype(jnp.bfloat16)
    grad_low = low_sums[:, rank:].astype(jnp.bfloat16)
    forward_sum = plain_dot(tokens_full, inner_weight)
    backward_sum = plain_dot(gated_full, outer_weight)
    pre = forward_sum + plain_dot(inner_low, inner_up) + inner_bias[None, :]
    hidden = gelu_value(pre).astype(jnp.bfloat16)
    grad_hidden = backward_sum + dot_rows(grad_low, outer_down)
    grad_pre = (grad_hidden * gelu_slope(pre)).astype(jnp.bfloat16)
    pre_low_part = dot_rows(grad_pre, inner_up)
    block_part = dot_rows(grad_pre, inner_weight).astype(jnp.bfloat16).astype(jnp.float32)
    low_part = dot_rows(pre_low_part.astype(jnp.bfloat16), inner_down)
    tokens_grad = lax.psum_scatter(
        (block_part + low_part).astype(jnp.bfloat16), "col", scatter_dimension=1, tiled=True
    )

    hidden_low_part = plain_dot(hidden, outer_down)
    lows = tree_sum(jnp.concatenate([hidden_low_part, pre_low_part], axis=1), "col", n_col)
    hidden_low = lows[:, :rank].astype(jnp.bfloat16)
    pre_low = lows[:, rank:].astype(jnp.bfloat16)

    scale = 1.0 / math.sqrt(tok_rows * n_row)
    outer_down_term = dot_cols(hidden, grad_low)
    outer_up_term = dot_cols(gated_local, hidden_low)
    inner_down_term = dot_cols(tokens_in, pre_low)
    inner_up_term = dot_cols(grad_pre, inner_low)
    packed = jnp.concatenate([outer_down_term, inner_up_term, outer_up_term, inner_down_term], axis=0)
    packed = tree_sum(packed, "row", n_row) * scale
    outer_down_grad = packed[:ff_local]
    inner_up_grad = packed[ff_local : 2 * ff_local].T
    outer_up_grad = packed[2 * ff_local : 2 * ff_local + local_width].T
    inner_down_grad = packed[2 * ff_local + local_width :]
    return (tokens_grad, inner_down_grad, inner_up_grad, outer_down_grad, outer_up_grad)


def solution(mesh):
    placed = (
        P("row", "col"),
        P("row", "col"),
        P(),
        P(None, "col"),
        P("col"),
        P(None, "col"),
        P(),
        P(None, "col"),
        P("col", None),
        P(),
    )
    return jax.shard_map(
        local,
        mesh=mesh,
        in_specs=placed,
        out_specs=(P("row", "col"), P("col", None), P(None, "col"), P("col", None), P(None, "col")),
        check_vma=False,
    )
```

```python
import math

import jax
import jax.numpy as jnp
from jax import lax
from jax.sharding import PartitionSpec as P

SLOPE_SCALE = 0.7978845608028654
CUBIC = 0.044715


def gelu_value(pre):
    inner = SLOPE_SCALE * (pre + CUBIC * pre * pre * pre)
    return 0.5 * pre * (1.0 + jnp.tanh(inner))


def gelu_slope(pre):
    tangent = jnp.tanh(SLOPE_SCALE * (pre + CUBIC * pre * pre * pre))
    return 0.5 * (1.0 + tangent) + 0.5 * pre * (1.0 - tangent * tangent) * SLOPE_SCALE * (
        1.0 + 3.0 * CUBIC * pre * pre
    )


def plain_dot(left, right):
    return jnp.dot(left, right, preferred_element_type=jnp.float32)


def dot_rows(left, right):
    return lax.dot_general(
        left, right, (((1,), (1,)), ((), ())), preferred_element_type=jnp.float32
    )


def dot_cols(left, right):
    return lax.dot_general(
        left, right, (((0,), (0,)), ((), ())), preferred_element_type=jnp.float32
    )


def tree_sum(value, axis, size):
    step = 1
    while step < size:
        pairs = [(i, i ^ step) for i in range(size)]
        value = value + lax.ppermute(value, axis, pairs)
        step *= 2
    return value


def local(
    tokens_in,
    token_grad,
    gate_gain,
    inner_weight,
    inner_bias,
    outer_weight,
    inner_down,
    inner_up,
    outer_down,
    outer_up,
):
    n_col = lax.axis_size("col")
    n_row = lax.axis_size("row")
    col_index = lax.axis_index("col")
    local_width = token_grad.shape[1]
    tok_rows = tokens_in.shape[0]
    ff_local = inner_weight.shape[1]
    rank = inner_down.shape[1]
    gain_local = lax.dynamic_slice_in_dim(gate_gain, col_index * local_width, local_width, 0)
    gated_local = (gain_local[None, :] * token_grad.astype(jnp.float32)).astype(jnp.bfloat16)
    both_full = lax.all_gather(jnp.stack([tokens_in, gated_local]), "col", axis=2, tiled=True)
    tokens_full, gated_full = both_full[0], both_full[1]
    inner_cat = jnp.concatenate([inner_weight, inner_down], axis=1)
    outer_cat = jnp.concatenate([outer_weight, outer_up.T], axis=1)
    forward_all = plain_dot(tokens_full, inner_cat)
    forward_sum = forward_all[:, :ff_local]
    inner_low = forward_all[:, ff_local:].astype(jnp.bfloat16)
    backward_all = plain_dot(gated_full, outer_cat)
    backward_sum = backward_all[:, :ff_local]
    grad_low = backward_all[:, ff_local:].astype(jnp.bfloat16)
    pre = forward_sum + plain_dot(inner_low, inner_up) + inner_bias[None, :]
    hidden = gelu_value(pre).astype(jnp.bfloat16)
    grad_hidden = backward_sum + dot_rows(grad_low, outer_down)
    grad_pre = (grad_hidden * gelu_slope(pre)).astype(jnp.bfloat16)
    pre_low_part = dot_rows(grad_pre, inner_up)
    grad_pre_cat = jnp.concatenate([grad_pre, pre_low_part.astype(jnp.bfloat16)], axis=1)
    block_part = dot_rows(grad_pre_cat, inner_cat).astype(jnp.bfloat16)
    tokens_grad = lax.psum_scatter(block_part, "col", scatter_dimension=1, tiled=True)

    hidden_low_part = plain_dot(hidden, outer_down)
    lows = tree_sum(jnp.concatenate([hidden_low_part, pre_low_part], axis=1), "col", n_col)
    hidden_low = lows[:, :rank].astype(jnp.bfloat16)
    pre_low = lows[:, rank:].astype(jnp.bfloat16)

    scale = 1.0 / math.sqrt(tok_rows * n_row)
    outer_down_term = dot_cols(hidden, grad_low)
    outer_up_term = dot_cols(gated_local, hidden_low)
    inner_down_term = dot_cols(tokens_in, pre_low)
    inner_up_term = dot_cols(grad_pre, inner_low)
    packed = jnp.concatenate([outer_down_term, inner_up_term, outer_up_term, inner_down_term], axis=0)
    packed = tree_sum(packed, "row", n_row) * scale
    outer_down_grad = packed[:ff_local]
    inner_up_grad = packed[ff_local : 2 * ff_local].T
    outer_up_grad = packed[2 * ff_local : 2 * ff_local + local_width].T
    inner_down_grad = packed[2 * ff_local + local_width :]
    return (tokens_grad, inner_down_grad, inner_up_grad, outer_down_grad, outer_up_grad)


def solution(mesh):
    placed = (
        P("row", "col"),
        P("row", "col"),
        P(),
        P(None, "col"),
        P("col"),
        P(None, "col"),
        P(),
        P(None, "col"),
        P("col", None),
        P(),
    )
    return jax.shard_map(
        local,
        mesh=mesh,
        in_specs=placed,
        out_specs=(P("row", "col"), P("col", None), P(None, "col"), P("col", None), P(None, "col")),
        check_vma=False,
    )
```

```python
import math

import jax
import jax.numpy as jnp
from jax import lax
from jax.sharding import PartitionSpec as P

SLOPE_SCALE = 0.7978845608028654
CUBIC = 0.044715


def gelu_value(pre):
    inner = SLOPE_SCALE * (pre + CUBIC * pre * pre * pre)
    return 0.5 * pre * (1.0 + jnp.tanh(inner))


def gelu_slope(pre):
    tangent = jnp.tanh(SLOPE_SCALE * (pre + CUBIC * pre * pre * pre))
    return 0.5 * (1.0 + tangent) + 0.5 * pre * (1.0 - tangent * tangent) * SLOPE_SCALE * (
        1.0 + 3.0 * CUBIC * pre * pre
    )


def plain_dot(left, right):
    return jnp.dot(left, right, preferred_element_type=jnp.float32)


def dot_rows(left, right):
    return lax.dot_general(
        left, right, (((1,), (1,)), ((), ())), preferred_element_type=jnp.float32
    )


def dot_cols(left, right):
    return lax.dot_general(
        left, right, (((0,), (0,)), ((), ())), preferred_element_type=jnp.float32
    )


def tree_sum(value, axis, size):
    step = 1
    while step < size:
        pairs = [(i, i ^ step) for i in range(size)]
        value = value + lax.ppermute(value, axis, pairs)
        step *= 2
    return value


def local(
    tokens_in,
    token_grad,
    gate_gain,
    inner_weight,
    inner_bias,
    outer_weight,
    inner_down,
    inner_up,
    outer_down,
    outer_up,
):
    n_col = lax.axis_size("col")
    n_row = lax.axis_size("row")
    col_index = lax.axis_index("col")
    local_width = token_grad.shape[1]
    tok_rows = tokens_in.shape[0]
    ff_local = inner_weight.shape[1]
    rank = inner_down.shape[1]
    gain_local = lax.dynamic_slice_in_dim(gate_gain, col_index * local_width, local_width, 0)
    gated_local = (gain_local[None, :] * token_grad.astype(jnp.float32)).astype(jnp.bfloat16)
    both_full = lax.all_gather(jnp.stack([tokens_in, gated_local]), "col", axis=2, tiled=True)
    tokens_full, gated_full = both_full[0], both_full[1]
    inner_cat = jnp.concatenate([inner_weight, inner_down], axis=1)
    outer_cat = jnp.concatenate([outer_weight, outer_up.T], axis=1)
    forward_all = plain_dot(tokens_full, inner_cat)
    forward_sum = forward_all[:, :ff_local]
    inner_low = forward_all[:, ff_local:].astype(jnp.bfloat16)
    backward_all = plain_dot(gated_full, outer_cat)
    backward_sum = backward_all[:, :ff_local]
    grad_low = backward_all[:, ff_local:].astype(jnp.bfloat16)
    pre = forward_sum + plain_dot(inner_low, inner_up) + inner_bias[None, :]
    hidden = gelu_value(pre).astype(jnp.bfloat16)
    grad_hidden = backward_sum + dot_rows(grad_low, outer_down)
    grad_pre = (grad_hidden * gelu_slope(pre)).astype(jnp.bfloat16)
    pre_low_part = dot_rows(grad_pre, inner_up)
    block_part = dot_rows(grad_pre, inner_weight).astype(jnp.bfloat16).astype(jnp.float32)
    low_part = dot_rows(pre_low_part.astype(jnp.bfloat16), inner_down)
    tokens_grad = lax.psum_scatter(
        (block_part + low_part).astype(jnp.bfloat16), "col", scatter_dimension=1, tiled=True
    )

    hidden_low_part = plain_dot(hidden, outer_down)
    lows = tree_sum(jnp.concatenate([hidden_low_part, pre_low_part], axis=1), "col", n_col)
    hidden_low = lows[:, :rank].astype(jnp.bfloat16)
    pre_low = lows[:, rank:].astype(jnp.bfloat16)

    scale = 1.0 / math.sqrt(tok_rows * n_row)
    outer_down_term = dot_cols(hidden, grad_low)
    outer_up_term = dot_cols(gated_local, hidden_low)
    inner_down_term = dot_cols(tokens_in, pre_low)
    inner_up_term = dot_cols(grad_pre, inner_low)
    packed = jnp.concatenate([outer_down_term, inner_up_term, outer_up_term, inner_down_term], axis=0)
    packed = tree_sum(packed, "row", n_row) * scale
    outer_down_grad = packed[:ff_local]
    inner_up_grad = packed[ff_local : 2 * ff_local].T
    outer_up_grad = packed[2 * ff_local : 2 * ff_local + local_width].T
    inner_down_grad = packed[2 * ff_local + local_width :]
    return (tokens_grad, inner_down_grad, inner_up_grad, outer_down_grad, outer_up_grad)


def solution(mesh):
    placed = (
        P("row", "col"),
        P("row", "col"),
        P(),
        P(None, "col"),
        P("col"),
        P(None, "col"),
        P(),
        P(None, "col"),
        P("col", None),
        P(),
    )
    return jax.shard_map(
        local,
        mesh=mesh,
        in_specs=placed,
        out_specs=(P("row", "col"), P("col", None), P(None, "col"), P("col", None), P(None, "col")),
        check_vma=False,
    )
```

```python
import math

import jax
import jax.numpy as jnp
from jax import lax
from jax.experimental import pallas as pl
from jax.experimental.pallas import tpu as pltpu
from jax.sharding import PartitionSpec as P

SLOPE_SCALE = 0.7978845608028654
CUBIC = 0.044715


def gelu_value(pre):
    inner = SLOPE_SCALE * (pre + CUBIC * pre * pre * pre)
    return 0.5 * pre * (1.0 + jnp.tanh(inner))


def gelu_slope(pre):
    tangent = jnp.tanh(SLOPE_SCALE * (pre + CUBIC * pre * pre * pre))
    return 0.5 * (1.0 + tangent) + 0.5 * pre * (1.0 - tangent * tangent) * SLOPE_SCALE * (
        1.0 + 3.0 * CUBIC * pre * pre
    )


def plain_dot(left, right):
    return jnp.dot(left, right, preferred_element_type=jnp.float32)


def dot_rows(left, right):
    return lax.dot_general(
        left, right, (((1,), (1,)), ((), ())), preferred_element_type=jnp.float32
    )


def dot_cols(left, right):
    return lax.dot_general(
        left, right, (((0,), (0,)), ((), ())), preferred_element_type=jnp.float32
    )


def tree_sum(value, axis, size):
    step = 1
    while step < size:
        pairs = [(i, i ^ step) for i in range(size)]
        value = value + lax.ppermute(value, axis, pairs)
        step *= 2
    return value


def block_kernel(weight_ref, grad_ref, down_ref, low_ref, out_ref):
    contract_rows = (((0,), (0,)), ((), ()))
    block = lax.dot_general(
        weight_ref[...], grad_ref[...], contract_rows, preferred_element_type=jnp.float32
    )
    low = lax.dot_general(down_ref[...], low_ref[...], contract_rows, preferred_element_type=jnp.float32)
    out_ref[...] = (block.astype(jnp.bfloat16).astype(jnp.float32) + low).astype(out_ref.dtype)


def block_product(weight_t, grad_t, down_t, low_t, tile=640):
    ff, features = weight_t.shape
    rank, tokens = low_t.shape
    return pl.pallas_call(
        block_kernel,
        out_shape=jax.ShapeDtypeStruct((features, tokens), jnp.bfloat16),
        grid=(features // tile,),
        in_specs=[
            pl.BlockSpec((ff, tile), lambda i: (0, i)),
            pl.BlockSpec((ff, tokens), lambda i: (0, 0)),
            pl.BlockSpec((rank, tile), lambda i: (0, i)),
            pl.BlockSpec((rank, tokens), lambda i: (0, 0)),
        ],
        out_specs=pl.BlockSpec((tile, tokens), lambda i: (i, 0)),
        cost_estimate=pl.CostEstimate(
            flops=2 * features * tokens * (ff + rank),
            transcendentals=0,
            bytes_accessed=2 * (ff * features + ff * tokens + features * tokens),
        ),
    )(weight_t, grad_t, down_t, low_t)


def local(
    tokens_in,
    token_grad,
    gate_gain,
    inner_weight,
    inner_bias,
    outer_weight,
    inner_down,
    inner_up,
    outer_down,
    outer_up,
):
    n_col = lax.axis_size("col")
    n_row = lax.axis_size("row")
    col_index = lax.axis_index("col")
    local_width = token_grad.shape[1]
    tok_rows = tokens_in.shape[0]
    ff_local = inner_weight.shape[1]
    rank = inner_down.shape[1]
    gain_local = lax.dynamic_slice_in_dim(gate_gain, col_index * local_width, local_width, 0)
    gated_local = (gain_local[None, :] * token_grad.astype(jnp.float32)).astype(jnp.bfloat16)
    both_full = lax.all_gather(jnp.stack([tokens_in, gated_local]), "col", axis=2, tiled=True)
    tokens_full, gated_full = both_full[0], both_full[1]
    inner_cat = jnp.concatenate([inner_weight, inner_down], axis=1)
    outer_cat = jnp.concatenate([outer_weight, outer_up.T], axis=1)
    forward_all = plain_dot(tokens_full, inner_cat)
    forward_sum = forward_all[:, :ff_local]
    inner_low = forward_all[:, ff_local:].astype(jnp.bfloat16)
    backward_all = plain_dot(gated_full, outer_cat)
    backward_sum = backward_all[:, :ff_local]
    grad_low = backward_all[:, ff_local:].astype(jnp.bfloat16)
    pre = forward_sum + plain_dot(inner_low, inner_up) + inner_bias[None, :]
    hidden = gelu_value(pre).astype(jnp.bfloat16)
    grad_hidden = backward_sum + dot_rows(grad_low, outer_down)
    grad_pre = (grad_hidden * gelu_slope(pre)).astype(jnp.bfloat16)
    pre_low_part = dot_rows(grad_pre, inner_up)
    block_t = block_product(inner_weight.T, grad_pre.T, inner_down.T, pre_low_part.astype(jnp.bfloat16).T)
    tokens_grad = lax.psum_scatter(block_t.T, "col", scatter_dimension=1, tiled=True)

    hidden_low_part = plain_dot(hidden, outer_down)
    lows = tree_sum(jnp.concatenate([hidden_low_part, pre_low_part], axis=1), "col", n_col)
    hidden_low = lows[:, :rank].astype(jnp.bfloat16)
    pre_low = lows[:, rank:].astype(jnp.bfloat16)

    scale = 1.0 / math.sqrt(tok_rows * n_row)
    outer_down_term = dot_cols(hidden, grad_low)
    outer_up_term = dot_cols(gated_local, hidden_low)
    inner_down_term = dot_cols(tokens_in, pre_low)
    inner_up_term = dot_cols(grad_pre, inner_low)
    packed = jnp.concatenate([outer_down_term, inner_up_term, outer_up_term, inner_down_term], axis=0)
    packed = tree_sum(packed, "row", n_row) * scale
    outer_down_grad = packed[:ff_local]
    inner_up_grad = packed[ff_local : 2 * ff_local].T
    outer_up_grad = packed[2 * ff_local : 2 * ff_local + local_width].T
    inner_down_grad = packed[2 * ff_local + local_width :]
    return (tokens_grad, inner_down_grad, inner_up_grad, outer_down_grad, outer_up_grad)


def solution(mesh):
    placed = (
        P("row", "col"),
        P("row", "col"),
        P(),
        P(None, "col"),
        P("col"),
        P(None, "col"),
        P(),
        P(None, "col"),
        P("col", None),
        P(),
    )
    return jax.shard_map(
        local,
        mesh=mesh,
        in_specs=placed,
        out_specs=(P("row", "col"), P("col", None), P(None, "col"), P("col", None), P(None, "col")),
        check_vma=False,
    )
```

```python
import math

import jax
import jax.numpy as jnp
from jax import lax
from jax.experimental import pallas as pl
from jax.experimental.pallas import tpu as pltpu
from jax.sharding import PartitionSpec as P

SLOPE_SCALE = 0.7978845608028654
CUBIC = 0.044715


def gelu_value(pre):
    inner = SLOPE_SCALE * (pre + CUBIC * pre * pre * pre)
    return 0.5 * pre * (1.0 + jnp.tanh(inner))


def gelu_slope(pre):
    tangent = jnp.tanh(SLOPE_SCALE * (pre + CUBIC * pre * pre * pre))
    return 0.5 * (1.0 + tangent) + 0.5 * pre * (1.0 - tangent * tangent) * SLOPE_SCALE * (
        1.0 + 3.0 * CUBIC * pre * pre
    )


def plain_dot(left, right):
    return jnp.dot(left, right, preferred_element_type=jnp.float32)


def dot_rows(left, right):
    return lax.dot_general(
        left, right, (((1,), (1,)), ((), ())), preferred_element_type=jnp.float32
    )


def dot_cols(left, right):
    return lax.dot_general(
        left, right, (((0,), (0,)), ((), ())), preferred_element_type=jnp.float32
    )


def tree_sum(value, axis, size):
    step = 1
    while step < size:
        pairs = [(i, i ^ step) for i in range(size)]
        value = value + lax.ppermute(value, axis, pairs)
        step *= 2
    return value


def block_kernel(weight_ref, grad_ref, down_ref, low_ref, out_ref):
    block = jnp.dot(weight_ref[...], grad_ref[...], preferred_element_type=jnp.float32)
    low = jnp.dot(down_ref[...], low_ref[...], preferred_element_type=jnp.float32)
    out_ref[...] = (block.astype(jnp.bfloat16).astype(jnp.float32) + low).astype(out_ref.dtype)


def block_product(weight, grad_t, down, low_t, tile=640):
    features, ff = weight.shape
    rank, tokens = low_t.shape
    return pl.pallas_call(
        block_kernel,
        out_shape=jax.ShapeDtypeStruct((features, tokens), jnp.bfloat16),
        grid=(features // tile,),
        in_specs=[
            pl.BlockSpec((tile, ff), lambda i: (i, 0)),
            pl.BlockSpec((ff, tokens), lambda i: (0, 0)),
            pl.BlockSpec((tile, rank), lambda i: (i, 0)),
            pl.BlockSpec((rank, tokens), lambda i: (0, 0)),
        ],
        out_specs=pl.BlockSpec((tile, tokens), lambda i: (i, 0)),
        cost_estimate=pl.CostEstimate(
            flops=2 * features * tokens * (ff + rank),
            transcendentals=0,
            bytes_accessed=2 * (ff * features + ff * tokens + features * tokens),
        ),
    )(weight, grad_t, down, low_t)


def local(
    tokens_in,
    token_grad,
    gate_gain,
    inner_weight,
    inner_bias,
    outer_weight,
    inner_down,
    inner_up,
    outer_down,
    outer_up,
):
    n_col = lax.axis_size("col")
    n_row = lax.axis_size("row")
    col_index = lax.axis_index("col")
    local_width = token_grad.shape[1]
    tok_rows = tokens_in.shape[0]
    ff_local = inner_weight.shape[1]
    rank = inner_down.shape[1]
    gain_local = lax.dynamic_slice_in_dim(gate_gain, col_index * local_width, local_width, 0)
    gated_local = (gain_local[None, :] * token_grad.astype(jnp.float32)).astype(jnp.bfloat16)
    both_full = lax.all_gather(jnp.stack([tokens_in, gated_local]), "col", axis=2, tiled=True)
    tokens_full, gated_full = both_full[0], both_full[1]
    inner_cat = jnp.concatenate([inner_weight, inner_down], axis=1)
    outer_cat = jnp.concatenate([outer_weight, outer_up.T], axis=1)
    forward_all = plain_dot(tokens_full, inner_cat)
    forward_sum = forward_all[:, :ff_local]
    inner_low = forward_all[:, ff_local:].astype(jnp.bfloat16)
    backward_all = plain_dot(gated_full, outer_cat)
    backward_sum = backward_all[:, :ff_local]
    grad_low = backward_all[:, ff_local:].astype(jnp.bfloat16)
    pre = forward_sum + plain_dot(inner_low, inner_up) + inner_bias[None, :]
    hidden = gelu_value(pre).astype(jnp.bfloat16)
    grad_hidden = backward_sum + dot_rows(grad_low, outer_down)
    grad_pre = (grad_hidden * gelu_slope(pre)).astype(jnp.bfloat16)
    pre_low_part = dot_rows(grad_pre, inner_up)
    block_t = block_product(inner_weight, grad_pre.T, inner_down, pre_low_part.astype(jnp.bfloat16).T)
    tokens_grad = lax.psum_scatter(block_t.T, "col", scatter_dimension=1, tiled=True)

    hidden_low_part = plain_dot(hidden, outer_down)
    lows = tree_sum(jnp.concatenate([hidden_low_part, pre_low_part], axis=1), "col", n_col)
    hidden_low = lows[:, :rank].astype(jnp.bfloat16)
    pre_low = lows[:, rank:].astype(jnp.bfloat16)

    scale = 1.0 / math.sqrt(tok_rows * n_row)
    outer_down_term = dot_cols(hidden, grad_low)
    outer_up_term = dot_cols(gated_local, hidden_low)
    inner_down_term = dot_cols(tokens_in, pre_low)
    inner_up_term = dot_cols(grad_pre, inner_low)
    packed = jnp.concatenate([outer_down_term, inner_up_term, outer_up_term, inner_down_term], axis=0)
    packed = tree_sum(packed, "row", n_row) * scale
    outer_down_grad = packed[:ff_local]
    inner_up_grad = packed[ff_local : 2 * ff_local].T
    outer_up_grad = packed[2 * ff_local : 2 * ff_local + local_width].T
    inner_down_grad = packed[2 * ff_local + local_width :]
    return (tokens_grad, inner_down_grad, inner_up_grad, outer_down_grad, outer_up_grad)


def solution(mesh):
    placed = (
        P("row", "col"),
        P("row", "col"),
        P(),
        P(None, "col"),
        P("col"),
        P(None, "col"),
        P(),
        P(None, "col"),
        P("col", None),
        P(),
    )
    return jax.shard_map(
        local,
        mesh=mesh,
        in_specs=placed,
        out_specs=(P("row", "col"), P("col", None), P(None, "col"), P("col", None), P(None, "col")),
        check_vma=False,
    )
```

```python
import math

import jax
import jax.numpy as jnp
from jax import lax
from jax.experimental import pallas as pl
from jax.experimental.pallas import tpu as pltpu
from jax.sharding import PartitionSpec as P

SLOPE_SCALE = 0.7978845608028654
CUBIC = 0.044715


def gelu_value(pre):
    inner = SLOPE_SCALE * (pre + CUBIC * pre * pre * pre)
    return 0.5 * pre * (1.0 + jnp.tanh(inner))


def gelu_slope(pre):
    tangent = jnp.tanh(SLOPE_SCALE * (pre + CUBIC * pre * pre * pre))
    return 0.5 * (1.0 + tangent) + 0.5 * pre * (1.0 - tangent * tangent) * SLOPE_SCALE * (
        1.0 + 3.0 * CUBIC * pre * pre
    )


def plain_dot(left, right):
    return jnp.dot(left, right, preferred_element_type=jnp.float32)


def dot_rows(left, right):
    return lax.dot_general(
        left, right, (((1,), (1,)), ((), ())), preferred_element_type=jnp.float32
    )


def dot_cols(left, right):
    return lax.dot_general(
        left, right, (((0,), (0,)), ((), ())), preferred_element_type=jnp.float32
    )


def tree_sum(value, axis, size):
    step = 1
    while step < size:
        pairs = [(i, i ^ step) for i in range(size)]
        value = value + lax.ppermute(value, axis, pairs)
        step *= 2
    return value


def block_kernel(weight_ref, grad_ref, down_ref, low_ref, out_ref):
    block = jnp.dot(weight_ref[...], grad_ref[...], preferred_element_type=jnp.float32)
    low = jnp.dot(down_ref[...], low_ref[...], preferred_element_type=jnp.float32)
    out_ref[...] = (block.astype(jnp.bfloat16).astype(jnp.float32) + low).astype(out_ref.dtype)


def block_product(weight, grad_t, down, low_t, tile=1280):
    features, ff = weight.shape
    rank, tokens = low_t.shape
    return pl.pallas_call(
        block_kernel,
        out_shape=jax.ShapeDtypeStruct((features, tokens), jnp.bfloat16),
        grid=(features // tile,),
        in_specs=[
            pl.BlockSpec((tile, ff), lambda i: (i, 0)),
            pl.BlockSpec((ff, tokens), lambda i: (0, 0)),
            pl.BlockSpec((tile, rank), lambda i: (i, 0)),
            pl.BlockSpec((rank, tokens), lambda i: (0, 0)),
        ],
        out_specs=pl.BlockSpec((tile, tokens), lambda i: (i, 0)),
        cost_estimate=pl.CostEstimate(
            flops=2 * features * tokens * (ff + rank),
            transcendentals=0,
            bytes_accessed=2 * (ff * features + ff * tokens + features * tokens),
        ),
    )(weight, grad_t, down, low_t)


def local(
    tokens_in,
    token_grad,
    gate_gain,
    inner_weight,
    inner_bias,
    outer_weight,
    inner_down,
    inner_up,
    outer_down,
    outer_up,
):
    n_col = lax.axis_size("col")
    n_row = lax.axis_size("row")
    col_index = lax.axis_index("col")
    local_width = token_grad.shape[1]
    tok_rows = tokens_in.shape[0]
    ff_local = inner_weight.shape[1]
    rank = inner_down.shape[1]
    gain_local = lax.dynamic_slice_in_dim(gate_gain, col_index * local_width, local_width, 0)
    gated_local = (gain_local[None, :] * token_grad.astype(jnp.float32)).astype(jnp.bfloat16)
    both_full = lax.all_gather(jnp.stack([tokens_in, gated_local]), "col", axis=2, tiled=True)
    tokens_full, gated_full = both_full[0], both_full[1]
    inner_cat = jnp.concatenate([inner_weight, inner_down], axis=1)
    outer_cat = jnp.concatenate([outer_weight, outer_up.T], axis=1)
    forward_all = plain_dot(tokens_full, inner_cat)
    forward_sum = forward_all[:, :ff_local]
    inner_low = forward_all[:, ff_local:].astype(jnp.bfloat16)
    backward_all = plain_dot(gated_full, outer_cat)
    backward_sum = backward_all[:, :ff_local]
    grad_low = backward_all[:, ff_local:].astype(jnp.bfloat16)
    pre = forward_sum + plain_dot(inner_low, inner_up) + inner_bias[None, :]
    hidden = gelu_value(pre).astype(jnp.bfloat16)
    grad_hidden = backward_sum + dot_rows(grad_low, outer_down)
    grad_pre = (grad_hidden * gelu_slope(pre)).astype(jnp.bfloat16)
    pre_low_part = dot_rows(grad_pre, inner_up)
    block_t = block_product(inner_weight, grad_pre.T, inner_down, pre_low_part.astype(jnp.bfloat16).T)
    tokens_grad = lax.psum_scatter(block_t.T, "col", scatter_dimension=1, tiled=True)

    hidden_low_part = plain_dot(hidden, outer_down)
    lows = tree_sum(jnp.concatenate([hidden_low_part, pre_low_part], axis=1), "col", n_col)
    hidden_low = lows[:, :rank].astype(jnp.bfloat16)
    pre_low = lows[:, rank:].astype(jnp.bfloat16)

    scale = 1.0 / math.sqrt(tok_rows * n_row)
    outer_down_term = dot_cols(hidden, grad_low)
    outer_up_term = dot_cols(gated_local, hidden_low)
    inner_down_term = dot_cols(tokens_in, pre_low)
    inner_up_term = dot_cols(grad_pre, inner_low)
    packed = jnp.concatenate([outer_down_term, inner_up_term, outer_up_term, inner_down_term], axis=0)
    packed = tree_sum(packed, "row", n_row) * scale
    outer_down_grad = packed[:ff_local]
    inner_up_grad = packed[ff_local : 2 * ff_local].T
    outer_up_grad = packed[2 * ff_local : 2 * ff_local + local_width].T
    inner_down_grad = packed[2 * ff_local + local_width :]
    return (tokens_grad, inner_down_grad, inner_up_grad, outer_down_grad, outer_up_grad)


def solution(mesh):
    placed = (
        P("row", "col"),
        P("row", "col"),
        P(),
        P(None, "col"),
        P("col"),
        P(None, "col"),
        P(),
        P(None, "col"),
        P("col", None),
        P(),
    )
    return jax.shard_map(
        local,
        mesh=mesh,
        in_specs=placed,
        out_specs=(P("row", "col"), P("col", None), P(None, "col"), P("col", None), P(None, "col")),
        check_vma=False,
    )
```

```python
import math

import jax
import jax.numpy as jnp
from jax import lax
from jax.experimental import pallas as pl
from jax.experimental.pallas import tpu as pltpu
from jax.sharding import PartitionSpec as P

SLOPE_SCALE = 0.7978845608028654
CUBIC = 0.044715


def gelu_value(pre):
    inner = SLOPE_SCALE * (pre + CUBIC * pre * pre * pre)
    return 0.5 * pre * (1.0 + jnp.tanh(inner))


def gelu_slope(pre):
    tangent = jnp.tanh(SLOPE_SCALE * (pre + CUBIC * pre * pre * pre))
    return 0.5 * (1.0 + tangent) + 0.5 * pre * (1.0 - tangent * tangent) * SLOPE_SCALE * (
        1.0 + 3.0 * CUBIC * pre * pre
    )


def plain_dot(left, right):
    return jnp.dot(left, right, preferred_element_type=jnp.float32)


def dot_rows(left, right):
    return lax.dot_general(
        left, right, (((1,), (1,)), ((), ())), preferred_element_type=jnp.float32
    )


def dot_cols(left, right):
    return lax.dot_general(
        left, right, (((0,), (0,)), ((), ())), preferred_element_type=jnp.float32
    )


def tree_sum(value, axis, size):
    step = 1
    while step < size:
        pairs = [(i, i ^ step) for i in range(size)]
        value = value + lax.ppermute(value, axis, pairs)
        step *= 2
    return value


def block_kernel(weight_ref, grad_ref, out_ref):
    block = jnp.dot(weight_ref[...], grad_ref[...], preferred_element_type=jnp.float32)
    out_ref[...] = block.astype(out_ref.dtype)


def block_product(weight, grad_t, tile=640):
    features, depth = weight.shape
    tokens = grad_t.shape[1]
    return pl.pallas_call(
        block_kernel,
        out_shape=jax.ShapeDtypeStruct((features, tokens), jnp.bfloat16),
        grid=(features // tile,),
        in_specs=[
            pl.BlockSpec((tile, depth), lambda i: (i, 0)),
            pl.BlockSpec((depth, tokens), lambda i: (0, 0)),
        ],
        out_specs=pl.BlockSpec((tile, tokens), lambda i: (i, 0)),
        cost_estimate=pl.CostEstimate(
            flops=2 * features * tokens * depth,
            transcendentals=0,
            bytes_accessed=2 * (depth * features + depth * tokens + features * tokens),
        ),
    )(weight, grad_t)


def local(
    tokens_in,
    token_grad,
    gate_gain,
    inner_weight,
    inner_bias,
    outer_weight,
    inner_down,
    inner_up,
    outer_down,
    outer_up,
):
    n_col = lax.axis_size("col")
    n_row = lax.axis_size("row")
    col_index = lax.axis_index("col")
    local_width = token_grad.shape[1]
    tok_rows = tokens_in.shape[0]
    ff_local = inner_weight.shape[1]
    rank = inner_down.shape[1]
    gain_local = lax.dynamic_slice_in_dim(gate_gain, col_index * local_width, local_width, 0)
    gated_local = (gain_local[None, :] * token_grad.astype(jnp.float32)).astype(jnp.bfloat16)
    both_full = lax.all_gather(jnp.stack([tokens_in, gated_local]), "col", axis=2, tiled=True)
    tokens_full, gated_full = both_full[0], both_full[1]
    inner_cat = jnp.concatenate([inner_weight, inner_down], axis=1)
    outer_cat = jnp.concatenate([outer_weight, outer_up.T], axis=1)
    forward_all = plain_dot(tokens_full, inner_cat)
    forward_sum = forward_all[:, :ff_local]
    inner_low = forward_all[:, ff_local:].astype(jnp.bfloat16)
    backward_all = plain_dot(gated_full, outer_cat)
    backward_sum = backward_all[:, :ff_local]
    grad_low = backward_all[:, ff_local:].astype(jnp.bfloat16)
    pre = forward_sum + plain_dot(inner_low, inner_up) + inner_bias[None, :]
    hidden = gelu_value(pre).astype(jnp.bfloat16)
    grad_hidden = backward_sum + dot_rows(grad_low, outer_down)
    grad_pre = (grad_hidden * gelu_slope(pre)).astype(jnp.bfloat16)
    pre_low_part = dot_rows(grad_pre, inner_up)
    block_t = block_product(
        inner_cat, jnp.concatenate([grad_pre.T, pre_low_part.astype(jnp.bfloat16).T], axis=0)
    )
    tokens_grad = lax.psum_scatter(block_t.T, "col", scatter_dimension=1, tiled=True)

    hidden_low_part = plain_dot(hidden, outer_down)
    lows = tree_sum(jnp.concatenate([hidden_low_part, pre_low_part], axis=1), "col", n_col)
    hidden_low = lows[:, :rank].astype(jnp.bfloat16)
    pre_low = lows[:, rank:].astype(jnp.bfloat16)

    scale = 1.0 / math.sqrt(tok_rows * n_row)
    outer_down_term = dot_cols(hidden, grad_low)
    outer_up_term = dot_cols(gated_local, hidden_low)
    inner_down_term = dot_cols(tokens_in, pre_low)
    inner_up_term = dot_cols(grad_pre, inner_low)
    packed = jnp.concatenate([outer_down_term, inner_up_term, outer_up_term, inner_down_term], axis=0)
    packed = tree_sum(packed, "row", n_row) * scale
    outer_down_grad = packed[:ff_local]
    inner_up_grad = packed[ff_local : 2 * ff_local].T
    outer_up_grad = packed[2 * ff_local : 2 * ff_local + local_width].T
    inner_down_grad = packed[2 * ff_local + local_width :]
    return (tokens_grad, inner_down_grad, inner_up_grad, outer_down_grad, outer_up_grad)


def solution(mesh):
    placed = (
        P("row", "col"),
        P("row", "col"),
        P(),
        P(None, "col"),
        P("col"),
        P(None, "col"),
        P(),
        P(None, "col"),
        P("col", None),
        P(),
    )
    return jax.shard_map(
        local,
        mesh=mesh,
        in_specs=placed,
        out_specs=(P("row", "col"), P("col", None), P(None, "col"), P("col", None), P(None, "col")),
        check_vma=False,
    )
```

```python
import math

import jax
import jax.numpy as jnp
from jax import lax
from jax.experimental import pallas as pl
from jax.experimental.pallas import tpu as pltpu
from jax.sharding import PartitionSpec as P

SLOPE_SCALE = 0.7978845608028654
CUBIC = 0.044715


def gelu_value(pre):
    inner = SLOPE_SCALE * (pre + CUBIC * pre * pre * pre)
    return 0.5 * pre * (1.0 + jnp.tanh(inner))


def gelu_slope(pre):
    tangent = jnp.tanh(SLOPE_SCALE * (pre + CUBIC * pre * pre * pre))
    return 0.5 * (1.0 + tangent) + 0.5 * pre * (1.0 - tangent * tangent) * SLOPE_SCALE * (
        1.0 + 3.0 * CUBIC * pre * pre
    )


def plain_dot(left, right):
    return jnp.dot(left, right, preferred_element_type=jnp.float32)


def dot_rows(left, right):
    return lax.dot_general(
        left, right, (((1,), (1,)), ((), ())), preferred_element_type=jnp.float32
    )


def dot_cols(left, right):
    return lax.dot_general(
        left, right, (((0,), (0,)), ((), ())), preferred_element_type=jnp.float32
    )


def tree_sum(value, axis, size):
    step = 1
    while step < size:
        pairs = [(i, i ^ step) for i in range(size)]
        value = value + lax.ppermute(value, axis, pairs)
        step *= 2
    return value


def block_kernel(weight_ref, grad_ref, out_ref):
    block = jnp.dot(weight_ref[...], grad_ref[...], preferred_element_type=jnp.float32)
    out_ref[...] = block.astype(out_ref.dtype)


def block_product(weight, grad_t, tile=640):
    features, depth = weight.shape
    tokens = grad_t.shape[1]
    return pl.pallas_call(
        block_kernel,
        out_shape=jax.ShapeDtypeStruct((features, tokens), jnp.bfloat16),
        grid=(features // tile,),
        in_specs=[
            pl.BlockSpec((tile, depth), lambda i: (i, 0)),
            pl.BlockSpec((depth, tokens), lambda i: (0, 0)),
        ],
        out_specs=pl.BlockSpec((tile, tokens), lambda i: (i, 0)),
        cost_estimate=pl.CostEstimate(
            flops=2 * features * tokens * depth,
            transcendentals=0,
            bytes_accessed=2 * (depth * features + depth * tokens + features * tokens),
        ),
    )(weight, grad_t)


def local(
    tokens_in,
    token_grad,
    gate_gain,
    inner_weight,
    inner_bias,
    outer_weight,
    inner_down,
    inner_up,
    outer_down,
    outer_up,
):
    n_col = lax.axis_size("col")
    n_row = lax.axis_size("row")
    col_index = lax.axis_index("col")
    local_width = token_grad.shape[1]
    tok_rows = tokens_in.shape[0]
    ff_local = inner_weight.shape[1]
    rank = inner_down.shape[1]
    gain_local = lax.dynamic_slice_in_dim(gate_gain, col_index * local_width, local_width, 0)
    gated_local = (gain_local[None, :] * token_grad.astype(jnp.float32)).astype(jnp.bfloat16)
    both_full = lax.all_gather(jnp.stack([tokens_in, gated_local]), "col", axis=2, tiled=True)
    tokens_full, gated_full = both_full[0], both_full[1]
    inner_cat = jnp.concatenate([inner_weight, inner_down], axis=1)
    outer_cat = jnp.concatenate([outer_weight, outer_up.T], axis=1)
    forward_all = plain_dot(tokens_full, inner_cat)
    forward_sum = forward_all[:, :ff_local]
    inner_low = forward_all[:, ff_local:].astype(jnp.bfloat16)
    backward_all = plain_dot(gated_full, outer_cat)
    backward_sum = backward_all[:, :ff_local]
    grad_low = backward_all[:, ff_local:].astype(jnp.bfloat16)
    pre = forward_sum + plain_dot(inner_low, inner_up) + inner_bias[None, :]
    hidden = gelu_value(pre).astype(jnp.bfloat16)
    grad_hidden = backward_sum + dot_rows(grad_low, outer_down)
    grad_pre = (grad_hidden * gelu_slope(pre)).astype(jnp.bfloat16)
    pre_low_part = dot_rows(grad_pre, inner_up)
    block_t = block_product(
        jnp.concatenate([inner_down, inner_weight], axis=1),
        jnp.concatenate([pre_low_part.astype(jnp.bfloat16).T, grad_pre.T], axis=0),
    )
    tokens_grad = lax.psum_scatter(block_t.T, "col", scatter_dimension=1, tiled=True)

    hidden_low_part = plain_dot(hidden, outer_down)
    lows = tree_sum(jnp.concatenate([hidden_low_part, pre_low_part], axis=1), "col", n_col)
    hidden_low = lows[:, :rank].astype(jnp.bfloat16)
    pre_low = lows[:, rank:].astype(jnp.bfloat16)

    scale = 1.0 / math.sqrt(tok_rows * n_row)
    outer_down_term = dot_cols(hidden, grad_low)
    outer_up_term = dot_cols(gated_local, hidden_low)
    inner_down_term = dot_cols(tokens_in, pre_low)
    inner_up_term = dot_cols(grad_pre, inner_low)
    packed = jnp.concatenate([outer_down_term, inner_up_term, outer_up_term, inner_down_term], axis=0)
    packed = tree_sum(packed, "row", n_row) * scale
    outer_down_grad = packed[:ff_local]
    inner_up_grad = packed[ff_local : 2 * ff_local].T
    outer_up_grad = packed[2 * ff_local : 2 * ff_local + local_width].T
    inner_down_grad = packed[2 * ff_local + local_width :]
    return (tokens_grad, inner_down_grad, inner_up_grad, outer_down_grad, outer_up_grad)


def solution(mesh):
    placed = (
        P("row", "col"),
        P("row", "col"),
        P(),
        P(None, "col"),
        P("col"),
        P(None, "col"),
        P(),
        P(None, "col"),
        P("col", None),
        P(),
    )
    return jax.shard_map(
        local,
        mesh=mesh,
        in_specs=placed,
        out_specs=(P("row", "col"), P("col", None), P(None, "col"), P("col", None), P(None, "col")),
        check_vma=False,
    )
```

```python
import math

import jax
import jax.numpy as jnp
from jax import lax
from jax.experimental import pallas as pl
from jax.experimental.pallas import tpu as pltpu
from jax.sharding import PartitionSpec as P

SLOPE_SCALE = 0.7978845608028654
CUBIC = 0.044715


def gelu_value(pre):
    inner = SLOPE_SCALE * (pre + CUBIC * pre * pre * pre)
    return 0.5 * pre * (1.0 + jnp.tanh(inner))


def gelu_slope(pre):
    tangent = jnp.tanh(SLOPE_SCALE * (pre + CUBIC * pre * pre * pre))
    return 0.5 * (1.0 + tangent) + 0.5 * pre * (1.0 - tangent * tangent) * SLOPE_SCALE * (
        1.0 + 3.0 * CUBIC * pre * pre
    )


def plain_dot(left, right):
    return jnp.dot(left, right, preferred_element_type=jnp.float32)


def dot_rows(left, right):
    return lax.dot_general(
        left, right, (((1,), (1,)), ((), ())), preferred_element_type=jnp.float32
    )


def dot_cols(left, right):
    return lax.dot_general(
        left, right, (((0,), (0,)), ((), ())), preferred_element_type=jnp.float32
    )


def tree_sum(value, axis, size):
    step = 1
    while step < size:
        pairs = [(i, i ^ step) for i in range(size)]
        value = value + lax.ppermute(value, axis, pairs)
        step *= 2
    return value


def block_kernel(weight_ref, grad_ref, out_ref):
    block = jnp.dot(weight_ref[...], grad_ref[...], preferred_element_type=jnp.float32)
    out_ref[...] = block.astype(out_ref.dtype)


def block_product(weight, grad_t, tile=1280):
    features, depth = weight.shape
    tokens = grad_t.shape[1]
    return pl.pallas_call(
        block_kernel,
        out_shape=jax.ShapeDtypeStruct((features, tokens), jnp.bfloat16),
        grid=(features // tile,),
        in_specs=[
            pl.BlockSpec((tile, depth), lambda i: (i, 0)),
            pl.BlockSpec((depth, tokens), lambda i: (0, 0)),
        ],
        out_specs=pl.BlockSpec((tile, tokens), lambda i: (i, 0)),
        cost_estimate=pl.CostEstimate(
            flops=2 * features * tokens * depth,
            transcendentals=0,
            bytes_accessed=2 * (depth * features + depth * tokens + features * tokens),
        ),
    )(weight, grad_t)


def local(
    tokens_in,
    token_grad,
    gate_gain,
    inner_weight,
    inner_bias,
    outer_weight,
    inner_down,
    inner_up,
    outer_down,
    outer_up,
):
    n_col = lax.axis_size("col")
    n_row = lax.axis_size("row")
    col_index = lax.axis_index("col")
    local_width = token_grad.shape[1]
    tok_rows = tokens_in.shape[0]
    ff_local = inner_weight.shape[1]
    rank = inner_down.shape[1]
    gain_local = lax.dynamic_slice_in_dim(gate_gain, col_index * local_width, local_width, 0)
    gated_local = (gain_local[None, :] * token_grad.astype(jnp.float32)).astype(jnp.bfloat16)
    both_full = lax.all_gather(jnp.stack([tokens_in, gated_local]), "col", axis=2, tiled=True)
    tokens_full, gated_full = both_full[0], both_full[1]
    inner_cat = jnp.concatenate([inner_weight, inner_down], axis=1)
    outer_cat = jnp.concatenate([outer_weight, outer_up.T], axis=1)
    forward_all = plain_dot(tokens_full, inner_cat)
    forward_sum = forward_all[:, :ff_local]
    inner_low = forward_all[:, ff_local:].astype(jnp.bfloat16)
    backward_all = plain_dot(gated_full, outer_cat)
    backward_sum = backward_all[:, :ff_local]
    grad_low = backward_all[:, ff_local:].astype(jnp.bfloat16)
    pre = forward_sum + plain_dot(inner_low, inner_up) + inner_bias[None, :]
    hidden = gelu_value(pre).astype(jnp.bfloat16)
    grad_hidden = backward_sum + dot_rows(grad_low, outer_down)
    grad_pre = (grad_hidden * gelu_slope(pre)).astype(jnp.bfloat16)
    pre_low_part = dot_rows(grad_pre, inner_up)
    block_t = block_product(
        jnp.concatenate([inner_down, inner_weight], axis=1),
        jnp.concatenate([pre_low_part.astype(jnp.bfloat16).T, grad_pre.T], axis=0),
    )
    tokens_grad = lax.psum_scatter(block_t.T, "col", scatter_dimension=1, tiled=True)

    hidden_low_part = plain_dot(hidden, outer_down)
    lows = tree_sum(jnp.concatenate([hidden_low_part, pre_low_part], axis=1), "col", n_col)
    hidden_low = lows[:, :rank].astype(jnp.bfloat16)
    pre_low = lows[:, rank:].astype(jnp.bfloat16)

    scale = 1.0 / math.sqrt(tok_rows * n_row)
    outer_down_term = dot_cols(hidden, grad_low)
    outer_up_term = dot_cols(gated_local, hidden_low)
    inner_down_term = dot_cols(tokens_in, pre_low)
    inner_up_term = dot_cols(grad_pre, inner_low)
    packed = jnp.concatenate([outer_down_term, inner_up_term, outer_up_term, inner_down_term], axis=0)
    packed = tree_sum(packed, "row", n_row) * scale
    outer_down_grad = packed[:ff_local]
    inner_up_grad = packed[ff_local : 2 * ff_local].T
    outer_up_grad = packed[2 * ff_local : 2 * ff_local + local_width].T
    inner_down_grad = packed[2 * ff_local + local_width :]
    return (tokens_grad, inner_down_grad, inner_up_grad, outer_down_grad, outer_up_grad)


def solution(mesh):
    placed = (
        P("row", "col"),
        P("row", "col"),
        P(),
        P(None, "col"),
        P("col"),
        P(None, "col"),
        P(),
        P(None, "col"),
        P("col", None),
        P(),
    )
    return jax.shard_map(
        local,
        mesh=mesh,
        in_specs=placed,
        out_specs=(P("row", "col"), P("col", None), P(None, "col"), P("col", None), P(None, "col")),
        check_vma=False,
    )
```

```python
import math

import jax
import jax.numpy as jnp
from jax import lax
from jax.experimental import pallas as pl
from jax.experimental.pallas import tpu as pltpu
from jax.sharding import PartitionSpec as P

SLOPE_SCALE = 0.7978845608028654
CUBIC = 0.044715


def gelu_value(pre):
    inner = SLOPE_SCALE * (pre + CUBIC * pre * pre * pre)
    return 0.5 * pre * (1.0 + jnp.tanh(inner))


def gelu_slope(pre):
    tangent = jnp.tanh(SLOPE_SCALE * (pre + CUBIC * pre * pre * pre))
    return 0.5 * (1.0 + tangent) + 0.5 * pre * (1.0 - tangent * tangent) * SLOPE_SCALE * (
        1.0 + 3.0 * CUBIC * pre * pre
    )


def plain_dot(left, right):
    return jnp.dot(left, right, preferred_element_type=jnp.float32)


def dot_rows(left, right):
    return lax.dot_general(
        left, right, (((1,), (1,)), ((), ())), preferred_element_type=jnp.float32
    )


def dot_cols(left, right):
    return lax.dot_general(
        left, right, (((0,), (0,)), ((), ())), preferred_element_type=jnp.float32
    )


def tree_sum(value, axis, size):
    step = 1
    while step < size:
        pairs = [(i, i ^ step) for i in range(size)]
        value = value + lax.ppermute(value, axis, pairs)
        step *= 2
    return value


def block_kernel(weight_ref, grad_ref, out_ref):
    block = jnp.dot(weight_ref[...], grad_ref[...], preferred_element_type=jnp.float32)
    out_ref[...] = block.astype(out_ref.dtype)


def block_product(weight, grad_t, tile=2560):
    features, depth = weight.shape
    tokens = grad_t.shape[1]
    return pl.pallas_call(
        block_kernel,
        out_shape=jax.ShapeDtypeStruct((features, tokens), jnp.bfloat16),
        grid=(features // tile,),
        in_specs=[
            pl.BlockSpec((tile, depth), lambda i: (i, 0)),
            pl.BlockSpec((depth, tokens), lambda i: (0, 0)),
        ],
        out_specs=pl.BlockSpec((tile, tokens), lambda i: (i, 0)),
        cost_estimate=pl.CostEstimate(
            flops=2 * features * tokens * depth,
            transcendentals=0,
            bytes_accessed=2 * (depth * features + depth * tokens + features * tokens),
        ),
    )(weight, grad_t)


def local(
    tokens_in,
    token_grad,
    gate_gain,
    inner_weight,
    inner_bias,
    outer_weight,
    inner_down,
    inner_up,
    outer_down,
    outer_up,
):
    n_col = lax.axis_size("col")
    n_row = lax.axis_size("row")
    col_index = lax.axis_index("col")
    local_width = token_grad.shape[1]
    tok_rows = tokens_in.shape[0]
    ff_local = inner_weight.shape[1]
    rank = inner_down.shape[1]
    gain_local = lax.dynamic_slice_in_dim(gate_gain, col_index * local_width, local_width, 0)
    gated_local = (gain_local[None, :] * token_grad.astype(jnp.float32)).astype(jnp.bfloat16)
    both_full = lax.all_gather(jnp.stack([tokens_in, gated_local]), "col", axis=2, tiled=True)
    tokens_full, gated_full = both_full[0], both_full[1]
    inner_cat = jnp.concatenate([inner_weight, inner_down], axis=1)
    outer_cat = jnp.concatenate([outer_weight, outer_up.T], axis=1)
    forward_all = plain_dot(tokens_full, inner_cat)
    forward_sum = forward_all[:, :ff_local]
    inner_low = forward_all[:, ff_local:].astype(jnp.bfloat16)
    backward_all = plain_dot(gated_full, outer_cat)
    backward_sum = backward_all[:, :ff_local]
    grad_low = backward_all[:, ff_local:].astype(jnp.bfloat16)
    pre = forward_sum + plain_dot(inner_low, inner_up) + inner_bias[None, :]
    hidden = gelu_value(pre).astype(jnp.bfloat16)
    grad_hidden = backward_sum + dot_rows(grad_low, outer_down)
    grad_pre = (grad_hidden * gelu_slope(pre)).astype(jnp.bfloat16)
    pre_low_part = dot_rows(grad_pre, inner_up)
    block_t = block_product(
        jnp.concatenate([inner_down, inner_weight], axis=1),
        jnp.concatenate([pre_low_part.astype(jnp.bfloat16).T, grad_pre.T], axis=0),
    )
    tokens_grad = lax.psum_scatter(block_t.T, "col", scatter_dimension=1, tiled=True)

    hidden_low_part = plain_dot(hidden, outer_down)
    lows = tree_sum(jnp.concatenate([hidden_low_part, pre_low_part], axis=1), "col", n_col)
    hidden_low = lows[:, :rank].astype(jnp.bfloat16)
    pre_low = lows[:, rank:].astype(jnp.bfloat16)

    scale = 1.0 / math.sqrt(tok_rows * n_row)
    outer_down_term = dot_cols(hidden, grad_low)
    outer_up_term = dot_cols(gated_local, hidden_low)
    inner_down_term = dot_cols(tokens_in, pre_low)
    inner_up_term = dot_cols(grad_pre, inner_low)
    packed = jnp.concatenate([outer_down_term, inner_up_term, outer_up_term, inner_down_term], axis=0)
    packed = tree_sum(packed, "row", n_row) * scale
    outer_down_grad = packed[:ff_local]
    inner_up_grad = packed[ff_local : 2 * ff_local].T
    outer_up_grad = packed[2 * ff_local : 2 * ff_local + local_width].T
    inner_down_grad = packed[2 * ff_local + local_width :]
    return (tokens_grad, inner_down_grad, inner_up_grad, outer_down_grad, outer_up_grad)


def solution(mesh):
    placed = (
        P("row", "col"),
        P("row", "col"),
        P(),
        P(None, "col"),
        P("col"),
        P(None, "col"),
        P(),
        P(None, "col"),
        P("col", None),
        P(),
    )
    return jax.shard_map(
        local,
        mesh=mesh,
        in_specs=placed,
        out_specs=(P("row", "col"), P("col", None), P(None, "col"), P("col", None), P(None, "col")),
        check_vma=False,
    )
```

```python
import math

import jax
import jax.numpy as jnp
from jax import lax
from jax.experimental import pallas as pl
from jax.experimental.pallas import tpu as pltpu
from jax.sharding import PartitionSpec as P

SLOPE_SCALE = 0.7978845608028654
CUBIC = 0.044715


def gelu_value(pre):
    inner = SLOPE_SCALE * (pre + CUBIC * pre * pre * pre)
    return 0.5 * pre * (1.0 + jnp.tanh(inner))


def gelu_slope(pre):
    tangent = jnp.tanh(SLOPE_SCALE * (pre + CUBIC * pre * pre * pre))
    return 0.5 * (1.0 + tangent) + 0.5 * pre * (1.0 - tangent * tangent) * SLOPE_SCALE * (
        1.0 + 3.0 * CUBIC * pre * pre
    )


def plain_dot(left, right):
    return jnp.dot(left, right, preferred_element_type=jnp.float32)


def dot_rows(left, right):
    return lax.dot_general(
        left, right, (((1,), (1,)), ((), ())), preferred_element_type=jnp.float32
    )


def dot_cols(left, right):
    return lax.dot_general(
        left, right, (((0,), (0,)), ((), ())), preferred_element_type=jnp.float32
    )


def tree_sum(value, axis, size):
    step = 1
    while step < size:
        pairs = [(i, i ^ step) for i in range(size)]
        value = value + lax.ppermute(value, axis, pairs)
        step *= 2
    return value


def block_kernel(weight_ref, grad_ref, down_ref, low_ref, out_ref):
    block = jnp.dot(weight_ref[...], grad_ref[...], preferred_element_type=jnp.float32)
    block += jnp.dot(down_ref[...], low_ref[...], preferred_element_type=jnp.float32)
    out_ref[...] = block.astype(out_ref.dtype)


def block_product(weight, grad_t, down, low_t, tile=1280):
    features, depth = weight.shape
    rank, tokens = low_t.shape
    return pl.pallas_call(
        block_kernel,
        out_shape=jax.ShapeDtypeStruct((features, tokens), jnp.bfloat16),
        grid=(features // tile,),
        in_specs=[
            pl.BlockSpec((tile, depth), lambda i: (i, 0)),
            pl.BlockSpec((depth, tokens), lambda i: (0, 0)),
            pl.BlockSpec((tile, rank), lambda i: (i, 0)),
            pl.BlockSpec((rank, tokens), lambda i: (0, 0)),
        ],
        out_specs=pl.BlockSpec((tile, tokens), lambda i: (i, 0)),
        cost_estimate=pl.CostEstimate(
            flops=2 * features * tokens * (depth + rank),
            transcendentals=0,
            bytes_accessed=2 * ((depth + rank) * (features + tokens) + features * tokens),
        ),
    )(weight, grad_t, down, low_t)


def local(
    tokens_in,
    token_grad,
    gate_gain,
    inner_weight,
    inner_bias,
    outer_weight,
    inner_down,
    inner_up,
    outer_down,
    outer_up,
):
    n_col = lax.axis_size("col")
    n_row = lax.axis_size("row")
    col_index = lax.axis_index("col")
    local_width = token_grad.shape[1]
    tok_rows = tokens_in.shape[0]
    ff_local = inner_weight.shape[1]
    rank = inner_down.shape[1]
    gain_local = lax.dynamic_slice_in_dim(gate_gain, col_index * local_width, local_width, 0)
    gated_local = (gain_local[None, :] * token_grad.astype(jnp.float32)).astype(jnp.bfloat16)
    both_full = lax.all_gather(jnp.stack([tokens_in, gated_local]), "col", axis=2, tiled=True)
    tokens_full, gated_full = both_full[0], both_full[1]
    inner_cat = jnp.concatenate([inner_weight, inner_down], axis=1)
    outer_cat = jnp.concatenate([outer_weight, outer_up.T], axis=1)
    forward_all = plain_dot(tokens_full, inner_cat)
    forward_sum = forward_all[:, :ff_local]
    inner_low = forward_all[:, ff_local:].astype(jnp.bfloat16)
    backward_all = plain_dot(gated_full, outer_cat)
    backward_sum = backward_all[:, :ff_local]
    grad_low = backward_all[:, ff_local:].astype(jnp.bfloat16)
    pre = forward_sum + plain_dot(inner_low, inner_up) + inner_bias[None, :]
    hidden = gelu_value(pre).astype(jnp.bfloat16)
    grad_hidden = backward_sum + dot_rows(grad_low, outer_down)
    grad_pre = (grad_hidden * gelu_slope(pre)).astype(jnp.bfloat16)
    pre_low_part = dot_rows(grad_pre, inner_up)
    block_t = block_product(
        inner_weight, grad_pre.T, inner_down, pre_low_part.astype(jnp.bfloat16).T
    )
    tokens_grad = lax.psum_scatter(block_t.T, "col", scatter_dimension=1, tiled=True)

    hidden_low_part = plain_dot(hidden, outer_down)
    lows = tree_sum(jnp.concatenate([hidden_low_part, pre_low_part], axis=1), "col", n_col)
    hidden_low = lows[:, :rank].astype(jnp.bfloat16)
    pre_low = lows[:, rank:].astype(jnp.bfloat16)

    scale = 1.0 / math.sqrt(tok_rows * n_row)
    outer_down_term = dot_cols(hidden, grad_low)
    outer_up_term = dot_cols(gated_local, hidden_low)
    inner_down_term = dot_cols(tokens_in, pre_low)
    inner_up_term = dot_cols(grad_pre, inner_low)
    packed = jnp.concatenate([outer_down_term, inner_up_term, outer_up_term, inner_down_term], axis=0)
    packed = tree_sum(packed, "row", n_row) * scale
    outer_down_grad = packed[:ff_local]
    inner_up_grad = packed[ff_local : 2 * ff_local].T
    outer_up_grad = packed[2 * ff_local : 2 * ff_local + local_width].T
    inner_down_grad = packed[2 * ff_local + local_width :]
    return (tokens_grad, inner_down_grad, inner_up_grad, outer_down_grad, outer_up_grad)


def solution(mesh):
    placed = (
        P("row", "col"),
        P("row", "col"),
        P(),
        P(None, "col"),
        P("col"),
        P(None, "col"),
        P(),
        P(None, "col"),
        P("col", None),
        P(),
    )
    return jax.shard_map(
        local,
        mesh=mesh,
        in_specs=placed,
        out_specs=(P("row", "col"), P("col", None), P(None, "col"), P("col", None), P(None, "col")),
        check_vma=False,
    )
```

```python
import math

import jax
import jax.numpy as jnp
from jax import lax
from jax.experimental import pallas as pl
from jax.experimental.pallas import tpu as pltpu
from jax.sharding import PartitionSpec as P

SLOPE_SCALE = 0.7978845608028654
CUBIC = 0.044715


def gelu_value(pre):
    inner = SLOPE_SCALE * (pre + CUBIC * pre * pre * pre)
    return 0.5 * pre * (1.0 + jnp.tanh(inner))


def gelu_slope(pre):
    tangent = jnp.tanh(SLOPE_SCALE * (pre + CUBIC * pre * pre * pre))
    return 0.5 * (1.0 + tangent) + 0.5 * pre * (1.0 - tangent * tangent) * SLOPE_SCALE * (
        1.0 + 3.0 * CUBIC * pre * pre
    )


def plain_dot(left, right):
    return jnp.dot(left, right, preferred_element_type=jnp.float32)


def dot_rows(left, right):
    return lax.dot_general(
        left, right, (((1,), (1,)), ((), ())), preferred_element_type=jnp.float32
    )


def dot_cols(left, right):
    return lax.dot_general(
        left, right, (((0,), (0,)), ((), ())), preferred_element_type=jnp.float32
    )


def tree_sum(value, axis, size):
    step = 1
    while step < size:
        pairs = [(i, i ^ step) for i in range(size)]
        value = value + lax.ppermute(value, axis, pairs)
        step *= 2
    return value


def block_kernel(weight_ref, grad_ref, out_ref):
    block = jnp.dot(weight_ref[...], grad_ref[...], preferred_element_type=jnp.float32)
    out_ref[...] = block.astype(out_ref.dtype)


def block_product(weight, grad_t, tile=1024):
    features, depth = weight.shape
    tokens = grad_t.shape[1]
    return pl.pallas_call(
        block_kernel,
        out_shape=jax.ShapeDtypeStruct((features, tokens), jnp.bfloat16),
        grid=(features // tile,),
        in_specs=[
            pl.BlockSpec((tile, depth), lambda i: (i, 0)),
            pl.BlockSpec((depth, tokens), lambda i: (0, 0)),
        ],
        out_specs=pl.BlockSpec((tile, tokens), lambda i: (i, 0)),
        cost_estimate=pl.CostEstimate(
            flops=2 * features * tokens * depth,
            transcendentals=0,
            bytes_accessed=2 * (depth * features + depth * tokens + features * tokens),
        ),
    )(weight, grad_t)


def local(
    tokens_in,
    token_grad,
    gate_gain,
    inner_weight,
    inner_bias,
    outer_weight,
    inner_down,
    inner_up,
    outer_down,
    outer_up,
):
    n_col = lax.axis_size("col")
    n_row = lax.axis_size("row")
    col_index = lax.axis_index("col")
    local_width = token_grad.shape[1]
    tok_rows = tokens_in.shape[0]
    ff_local = inner_weight.shape[1]
    rank = inner_down.shape[1]
    gain_local = lax.dynamic_slice_in_dim(gate_gain, col_index * local_width, local_width, 0)
    gated_local = (gain_local[None, :] * token_grad.astype(jnp.float32)).astype(jnp.bfloat16)
    both_full = lax.all_gather(jnp.stack([tokens_in, gated_local]), "col", axis=2, tiled=True)
    tokens_full, gated_full = both_full[0], both_full[1]
    inner_cat = jnp.concatenate([inner_weight, inner_down], axis=1)
    outer_cat = jnp.concatenate([outer_weight, outer_up.T], axis=1)
    forward_all = plain_dot(tokens_full, inner_cat)
    forward_sum = forward_all[:, :ff_local]
    inner_low = forward_all[:, ff_local:].astype(jnp.bfloat16)
    backward_all = plain_dot(gated_full, outer_cat)
    backward_sum = backward_all[:, :ff_local]
    grad_low = backward_all[:, ff_local:].astype(jnp.bfloat16)
    pre = forward_sum + plain_dot(inner_low, inner_up) + inner_bias[None, :]
    hidden = gelu_value(pre).astype(jnp.bfloat16)
    grad_hidden = backward_sum + dot_rows(grad_low, outer_down)
    grad_pre = (grad_hidden * gelu_slope(pre)).astype(jnp.bfloat16)
    pre_low_part = dot_rows(grad_pre, inner_up)
    block_t = block_product(
        jnp.concatenate([inner_down, inner_weight], axis=1),
        jnp.concatenate([pre_low_part.astype(jnp.bfloat16).T, grad_pre.T], axis=0),
    )
    tokens_grad = lax.psum_scatter(block_t.T, "col", scatter_dimension=1, tiled=True)

    hidden_low_part = plain_dot(hidden, outer_down)
    lows = tree_sum(jnp.concatenate([hidden_low_part, pre_low_part], axis=1), "col", n_col)
    hidden_low = lows[:, :rank].astype(jnp.bfloat16)
    pre_low = lows[:, rank:].astype(jnp.bfloat16)

    scale = 1.0 / math.sqrt(tok_rows * n_row)
    outer_down_term = dot_cols(hidden, grad_low)
    outer_up_term = dot_cols(gated_local, hidden_low)
    inner_down_term = dot_cols(tokens_in, pre_low)
    inner_up_term = dot_cols(grad_pre, inner_low)
    packed = jnp.concatenate([outer_down_term, inner_up_term, outer_up_term, inner_down_term], axis=0)
    packed = tree_sum(packed, "row", n_row) * scale
    outer_down_grad = packed[:ff_local]
    inner_up_grad = packed[ff_local : 2 * ff_local].T
    outer_up_grad = packed[2 * ff_local : 2 * ff_local + local_width].T
    inner_down_grad = packed[2 * ff_local + local_width :]
    return (tokens_grad, inner_down_grad, inner_up_grad, outer_down_grad, outer_up_grad)


def solution(mesh):
    placed = (
        P("row", "col"),
        P("row", "col"),
        P(),
        P(None, "col"),
        P("col"),
        P(None, "col"),
        P(),
        P(None, "col"),
        P("col", None),
        P(),
    )
    return jax.shard_map(
        local,
        mesh=mesh,
        in_specs=placed,
        out_specs=(P("row", "col"), P("col", None), P(None, "col"), P("col", None), P(None, "col")),
        check_vma=False,
    )
```
